32 devices in a mesh: orb: 8 (over y, x, core), grid: 4 (over z).
Axes of the slice: x: 2, y: 2, z: 4, core: 2. Of those that a mesh axis runs over, the one named last changes fastest.
Arguments:
- ground_orbitals: float32 [32, 81000], P('orb'), may hold values from -6 to 6
- occupation_signs: int32 [32], P('orb'), may hold values from -1 to 1, as said below
- response_orbitals: float32 [32, 81000], P(('orb', 'grid')), may hold values from -1.5 to 1.5
- window_offsets: int32 [32, 2], P(('orb', 'grid')), may hold values from 0 to 3
- ground_density: float32 [81000], replicated, may hold values from 0.5 to 4
Outputs:
- response_action: float32 [32, 81000], P(('orb', 'grid'))
The draws below stay inside these ranges and needn't reach their ends.
Inputs may be any that keep to these rules, and one draw needn't show every extreme that they name: `occupation_signs`: every entry is -1 or +1.
All inputs are finite; a program needn't handle non-finite values.
Results may differ from the reference program's by a relative error of at most 0.0003.
Values sent between devices are 32-bit elements; how exact they have to be, the bound alone decides.
No kernel may reach another device: no remote copies, remote signals or barrier semaphores. Data moves between devices by JAX's collectives and lax.ppermute only.
A program may use at most 128 MiB of HBM per device.

```python
import math
import jax
import jax.numpy as jnp
from jax import lax

NX = 30
NY = 45
NZ = 60
CYCLE = 2
G = 81000
NB = 4
NORB = 32
N_ORB = 8


def draw_occupation_signs(key, part):
    return (2 * jax.random.randint(key, (NORB,), 0, 2) - 1).astype(jnp.int32)


def plant(array, rng, low, high):
    dims = array.shape
    spot = [jax.random.randint(jax.random.fold_in(rng, axis), (), 0, dims[axis]) for axis in range(len(dims))]
    array = array.at[tuple(spot)].set(low)
    longest = dims.index(max(dims))
    spot[longest] = (spot[longest] + 1) % dims[longest]
    return array.at[tuple(spot)].set(high)


def block_scale(stream_key, shape, cuts, smallest, largest):
    gain, own = 1.0, jax.random.fold_in(stream_key, 6)
    for axis_at, shards_of in cuts:
        steps = jnp.exp(jax.random.uniform(jax.random.fold_in(own, axis_at), (shards_of,), jnp.float32, smallest / len(cuts), largest / len(cuts)))
        gain = gain * jnp.repeat(steps, shape[axis_at] // shards_of).reshape([-1 if axis == axis_at else 1 for axis in range(len(shape))])
    return gain


def scatter_about(key, shape, deviation, limit, split=(), dtype=jnp.bfloat16):
    result = jax.random.normal(key, shape, jnp.float32) * deviation
    if len(split) > 0:
        result = block_scale(key, shape, split, -0.22, 0.18) * result
    return jnp.clip(result, min=-limit, max=limit).astype(dtype)


def setup_inputs(seed: int = 0) -> dict:
    key_list = jax.random.split(jax.random.key(seed), 6)
    ground_orbitals = scatter_about(key_list[0], (NORB, G), 1.0, 6.0, ((0, 8),), jnp.float32)
    occupation_signs = draw_occupation_signs(jax.random.fold_in(key_list[5], 71), 0)
    response_orbitals = scatter_about(key_list[2], (NORB, G), 0.25, 1.5, ((0, 32),), jnp.float32)
    window_offsets = plant(jax.random.randint(key_list[3], (NORB, CYCLE), 0, NB), jax.random.fold_in(key_list[3], 1), 0, NB - 1).astype(jnp.int32)
    ground_density = jnp.clip(jnp.exp(jax.random.uniform(key_list[4], (G,), jnp.float32, math.log(0.5), math.log(4.0))), 0.5, 4.0)
    return {"ground_orbitals": ground_orbitals, "occupation_signs": occupation_signs, "response_orbitals": response_orbitals, "window_offsets": window_offsets, "ground_density": ground_density}


SPACING = 0.5
SCREEN = 0.5
XC_COEF = 0.3282
HYBRID = 0.25


def wave_numbers(count):
    positions = jnp.arange(count)
    folded = jnp.where(positions <= count // 2, positions, positions - count)
    return folded.astype(jnp.float32) * (2.0 * math.pi / (count * SPACING))


def coulomb_kernel():
    wave_x = wave_numbers(NX)
    wave_y = wave_numbers(NY)
    wave_z = wave_numbers(NZ)
    squared = wave_x[:, None, None] ** 2 + wave_y[None, :, None] ** 2 + wave_z[None, None, :] ** 2
    return 4.0 * math.pi / (squared + SCREEN * SCREEN)


def poisson(pair, kernel):
    return jnp.real(jnp.fft.ifftn(jnp.fft.fftn(pair) * kernel))


def reference(ground_orbitals, occupation_signs, response_orbitals, window_offsets, ground_density):
    kernel = coulomb_kernel()
    signs = occupation_signs.astype(jnp.float32)
    block_ids = jnp.arange(NB).astype(jnp.int32)

    def single_orbital(orbital):
        response = response_orbitals[orbital].reshape(NX, NY, NZ)
        block_index = orbital // NB

        def cycle_turn(total, cycle_step):
            source = (block_index - cycle_step) % N_ORB
            start = (source * NB).astype(jnp.int32)
            phis = lax.dynamic_slice_in_dim(ground_orbitals, start, NB, 0).reshape(NB, NX, NY, NZ)
            block_signs = lax.dynamic_slice_in_dim(signs, start, NB, 0)
            keep = (block_ids >= window_offsets[orbital, cycle_step]).astype(jnp.float32)
            potentials = jax.vmap(poisson, (0, None))(phis * response[None], kernel)
            weight = (block_signs * keep)[:, None, None, None]
            return total + jnp.sum(weight * phis * potentials, 0), None

        total, _ = lax.scan(cycle_turn, jnp.zeros((NX, NY, NZ), jnp.float32), jnp.arange(CYCLE).astype(jnp.int32))
        return total.reshape(NX * NY * NZ)

    exchange = lax.map(single_orbital, jnp.arange(NORB).astype(jnp.int32))
    density = jnp.sum(signs[:, None] * ground_orbitals * response_orbitals, 0)
    potential = (-XC_COEF * ground_density ** (-2.0 / 3.0)) * density
    return potential[None, :] * ground_orbitals - HYBRID * exchange
```

```python
import functools
import math

import numpy as np

import jax
import jax.numpy as jnp
from jax import lax
from jax.experimental import pallas as pl
from jax.experimental.pallas import tpu as pltpu
from jax.sharding import PartitionSpec as P

NX = 30
NY = 45
NZ = 60
SPACING = 0.5
SCREEN = 0.5
XC_COEF = 0.3282
HYBRID = 0.25

F32 = jnp.float32
BF16 = jnp.bfloat16
LANES = 128
POINTS = NX * NY * NZ
XP = 32
YP = 48
ZP = LANES // 2
LINES = math.lcm(NZ, LANES) // NZ
CHUNKS = math.lcm(NZ, LANES) // LANES
PERIODS = -(-NX * NY // LINES)
LINE_ROWS = PERIODS * LINES
FLAT_ROWS = PERIODS * CHUNKS
WHOLE = POINTS // LANES
TAIL = POINTS - WHOLE * LANES
SENT_ROWS = 640


def real_basis(count):
    waves = np.arange(count)
    folded = np.where(waves <= count // 2, waves, count - waves)
    angle = 2.0 * np.pi * np.outer(folded, waves) / count
    basis = np.where((waves <= count // 2)[:, None], np.cos(angle), np.sin(angle))
    return basis / np.sqrt(np.sum(basis**2, 1, keepdims=True))


def split_table(table):
    table = table.astype(np.float32)
    high = table.astype(jnp.bfloat16)
    return high, (table - high.astype(np.float32)).astype(jnp.bfloat16)


def padded(table, size):
    return np.pad(table, ((0, size - table.shape[0]), (0, size - table.shape[1])))


def lane_table(matrix):
    high, low = (np.kron(np.eye(2, dtype=jnp.bfloat16), padded(part, ZP)) for part in split_table(matrix))
    return np.block([[high, low], [high, np.zeros_like(low)]])


def row_table(matrix, size):
    high, low = (padded(part, size) for part in split_table(matrix))
    return np.concatenate([high, high, low], 1)


def kernel_table():
    def squares(count):
        places = np.arange(count)
        folded = np.where(places <= count // 2, places, places - count)
        waves = folded.astype(np.float32) * np.float32(2.0 * math.pi / (count * SPACING))
        return waves * waves

    squared = squares(NX)[None, :, None] + squares(NY)[:, None, None] + squares(NZ)[None, None, :]
    table = np.zeros((YP, XP, 2, ZP), np.float32)
    table[:NY, :NX, :, :NZ] = (4.0 * math.pi / (squared + SCREEN * SCREEN))[:, :, None, :]
    return table.reshape(YP * XP, LANES)


def split(values):
    high = values.astype(BF16)
    return high, (values - high.astype(F32)).astype(BF16)


def lane_product(values, table):
    high, low = split(values)
    halves = []
    for start in range(0, values.shape[1], LANES):
        lanes = slice(start, start + LANES)
        both = jnp.dot(jnp.concatenate([high[:, lanes], low[:, lanes]], 1), table, preferred_element_type=F32)
        halves.append(both[:, :LANES] + both[:, LANES:])
    return jnp.concatenate(halves, 1)


def row_product(table, values):
    high, low = split(values)
    return jnp.dot(table, jnp.concatenate([high, low, high], 0), preferred_element_type=F32)


def lane_ids(rows):
    return lax.broadcasted_iota(jnp.int32, (rows, LANES), 1)


def turned(values, shift):
    shift %= LANES
    return pltpu.roll(values, shift, 1) if shift else values


def line_of(flat, line, place):
    chunk, start = divmod(NZ * line, LANES)
    first = turned(flat[pl.ds(chunk, PERIODS, stride=CHUNKS), :], place - start)
    if start + NZ <= LANES:
        return first
    second = turned(flat[pl.ds(chunk + 1, PERIODS, stride=CHUNKS), :], place - start)
    return jnp.where(lane_ids(PERIODS) < place + LANES - start, first, second)


def to_lines(left, right, lines):
    ids = lane_ids(PERIODS)
    for line in range(LINES):
        low, high = line_of(left, line, 0), line_of(right, line, ZP)
        both = jnp.where(ids < NZ, low, jnp.where((ids >= ZP) & (ids < ZP + NZ), high, 0.0))
        lines[pl.ds(line, PERIODS, stride=LINES), :] = both


def to_flat(lines, flat):
    ids = lane_ids(PERIODS)
    for chunk in range(CHUNKS):
        low = chunk * LANES
        merged = None
        for line in range(low // NZ, -(-(low + LANES) // NZ)):
            value = turned(lines[pl.ds(line, PERIODS, stride=LINES), :], NZ * line - low)
            merged = value if merged is None else jnp.where(ids >= NZ * line - low, value, merged)
        flat[pl.ds(chunk, PERIODS, stride=CHUNKS), :] = merged


def fill_flat(row, flat):
    flat[pl.ds(0, WHOLE), :] = row.at[:, pl.ds(0, WHOLE * LANES)].reshape(WHOLE, LANES)[...]
    flat[pl.ds(WHOLE, flat.shape[0] - WHOLE), :] = jnp.zeros((flat.shape[0] - WHOLE, LANES), F32)
    flat[pl.ds(WHOLE, 1), pl.ds(0, TAIL)] = row[:, pl.ds(WHOLE * LANES, TAIL)]


def grouped(count, group, body):
    lax.fori_loop(0, count // group, lambda step, carry: (body(step * group), carry)[1], 0)


def prelude_kernel(position, signs, offsets, ground, response, term, own, kept, sent, row_g, row_r, sems):
    place = position[0]
    copies = [
        pltpu.make_async_copy(ground.at[pl.ds(place, 1), :], row_g, sems.at[0]),
        pltpu.make_async_copy(response, row_r, sems.at[1]),
    ]
    for copy in copies:
        copy.start()
    for copy in copies:
        copy.wait()
    fill_flat(row_g, own)
    fill_flat(row_r, kept)
    term[...] = signs[place].astype(F32) * own[...] * kept[...]
    sent[...] = kept[...]
    last = pl.ds(SENT_ROWS - 1, 1)
    kept[last, :] = jnp.full((1, LANES), offsets[0, 0].astype(F32))
    sent[last, :] = jnp.full((1, LANES), offsets[0, 1].astype(F32))


def lines_kernel(ground, lines, rows, flats, sems):
    copies = [
        pltpu.make_async_copy(ground.at[pl.ds(j, 1), :], rows.at[j], sems.at[j]) for j in range(4)
    ]
    for copy in copies:
        copy.start()
    for j in range(4):
        copies[j].wait()
        fill_flat(rows.at[j], flats.at[j])
    for half in range(2):
        to_lines(flats.at[2 * half], flats.at[2 * half + 1], lines.at[half])


def coefficient_kernel(density, own, coefficient, flat):
    fill_flat(density, flat)
    spots = lax.broadcasted_iota(jnp.int32, (SENT_ROWS, LANES), 0) * LANES + lane_ids(SENT_ROWS)
    values = jnp.where(spots < POINTS, flat[...], 1.0)
    coefficient[...] = -XC_COEF * jnp.exp(jnp.log(values) * (-2.0 / 3.0)) * own[...]


def forward_kernel(lines, response, z_table, y_table, waves, flat, response_lines):
    flat[pl.ds(0, WHOLE + 1), :] = response[pl.ds(0, WHOLE + 1), :]
    flat[pl.ds(WHOLE + 1, FLAT_ROWS - WHOLE - 1), :] = jnp.zeros((FLAT_ROWS - WHOLE - 1, LANES), F32)
    to_lines(flat, flat, response_lines)
    for half in range(2):
        for x in range(NX, XP):
            waves[half, pl.ds(x, YP, stride=XP), :] = jnp.zeros((YP, LANES), F32)
    z_weights, y_weights = z_table[...], y_table[...]
    group = 15

    def body(x):
        products = []
        for u in range(group):
            spot = pl.ds((x + u) * NY, YP)
            value = response_lines[spot, :]
            products.append(jnp.concatenate([lines[0, spot, :] * value, lines[1, spot, :] * value], 1))
        values = lane_product(jnp.concatenate(products, 0), z_weights)
        values = jnp.concatenate([values[u * YP : (u + 1) * YP] for u in range(group)], 1)
        values = row_product(y_weights, values)
        for u in range(group):
            for half in range(2):
                start = (2 * u + half) * LANES
                waves[half, pl.ds(x + u, YP, stride=XP), :] = values[:, start : start + LANES]

    grouped(NX, group, body)


def middle_kernel(waves, kernel, forward_table, inverse_table, out):
    for half in range(2):
        for y in range(NY, YP):
            out[half, pl.ds(y, XP, stride=YP), :] = jnp.zeros((XP, LANES), F32)
    forward, inverse = forward_table[...], inverse_table[...]
    group = 15

    def body(y):
        values, factors = [], []
        for u in range(group):
            spot = pl.ds(pl.multiple_of((y + u) * XP, XP), XP)
            factor = kernel[spot, :]
            values += [waves[0, spot, :], waves[1, spot, :]]
            factors += [factor, factor]
        value = row_product(forward, jnp.concatenate(values, 1))
        value = row_product(inverse, value * jnp.concatenate(factors, 1))
        for u in range(group):
            for half in range(2):
                start = (2 * u + half) * LANES
                out[half, pl.ds(y + u, XP, stride=YP), :] = value[:, start : start + LANES]

    grouped(NY, group, body)


def inverse_kernel(signs, waves, lines, response, y_table, z_table, exchange, total, flat, offset, sem):
    copy = pltpu.make_async_copy(response.at[pl.ds(SENT_ROWS - 8, 8), :], offset, sem)
    copy.start()
    copy.wait()
    z_weights, y_weights = z_table[...], y_table[...]
    ids = lane_ids(1)
    factors = []
    for half in range(2):
        orbital = 2 * half + (ids >= ZP).astype(jnp.int32)
        sign = jnp.where(ids < ZP, signs[2 * half].astype(F32), signs[2 * half + 1].astype(F32))
        factors.append(jnp.where(orbital.astype(F32) >= offset[7:8, :], sign, 0.0))
    group = 15

    def body(x):
        values = []
        for u in range(group):
            spot = pl.ds(pl.multiple_of((x + u) * YP, YP), YP)
            values += [waves[0, spot, :], waves[1, spot, :]]
        value = row_product(y_weights, jnp.concatenate(values, 1))
        value = jnp.concatenate([value[:, 2 * u * LANES : 2 * (u + 1) * LANES] for u in range(group)], 0)
        value = lane_product(value, z_weights)
        for u in range(group):
            spot = pl.ds((x + u) * NY, YP)
            rows = value[u * YP : (u + 1) * YP]
            summed = rows[:, :LANES] * (lines[0, spot, :] * factors[0])
            summed += rows[:, LANES:] * (lines[1, spot, :] * factors[1])
            total[spot, :] = summed + pltpu.roll(summed, ZP, 1)

    grouped(NX, group, body)
    to_flat(total, flat)
    exchange[...] = flat[pl.ds(0, SENT_ROWS), :]


def finish_kernel(coefficient, density, first, second, out):
    value = coefficient[...] * density[...] - HYBRID * (first[...] + second[...])
    out.at[:, pl.ds(0, WHOLE * LANES)].reshape(WHOLE, LANES)[...] = value[:WHOLE]
    out[:, pl.ds(WHOLE * LANES, TAIL)] = value[WHOLE : WHOLE + 1, :TAIL]


SCALARS = pl.BlockSpec(memory_space=pltpu.SMEM)
VECTORS = pl.BlockSpec(memory_space=pltpu.VMEM)
ANYWHERE = pl.BlockSpec(memory_space=pl.ANY)


def call(body, name, specs, shapes, scratch, microseconds, outs=None):
    cost = pl.CostEstimate(flops=int(microseconds * 1e9), bytes_accessed=int(microseconds * 1e6), transcendentals=0)
    return pl.pallas_call(
        body,
        name=name,
        in_specs=specs,
        out_shape=[jax.ShapeDtypeStruct(shape, F32) for shape in shapes],
        out_specs=[VECTORS] * len(shapes),
        scratch_shapes=scratch,
        cost_estimate=cost,
    )


def swap(values, axis, distance):
    count = lax.axis_size(axis)
    return lax.ppermute(values, axis, [(i, i ^ distance) for i in range(count)])


def summed_over_devices(term):
    orb_bits = [("orb", 1 << bit) for bit in range(lax.axis_size("orb").bit_length() - 1)]
    grid_bits = [("grid", 1 << bit) for bit in range(lax.axis_size("grid").bit_length() - 1)]
    split_bits, rest = orb_bits[:2], orb_bits[2:] + grid_bits
    for axis, distance in split_bits:
        bit = (lax.axis_index(axis) // distance) % 2
        pair = term.reshape(2, term.shape[0] // 2, LANES)
        kept = lax.dynamic_index_in_dim(pair, bit, 0, keepdims=False)
        sent = lax.dynamic_index_in_dim(pair, 1 - bit, 0, keepdims=False)
        term = kept + swap(sent, axis, distance)
    for axis, distance in rest:
        term = term + swap(term, axis, distance)
    for axis, distance in split_bits[::-1]:
        bit = (lax.axis_index(axis) // distance) % 2
        other = swap(term, axis, distance)
        term = jnp.concatenate([jnp.where(bit == 0, term, other), jnp.where(bit == 0, other, term)], 0)
    return term


def exchange_of(signs, lines, response, tables):
    waves = call(
        forward_kernel, "forward", [VECTORS] * 4, [(2, YP * XP, LANES)],
        [pltpu.VMEM((FLAT_ROWS, LANES), F32), pltpu.VMEM((LINE_ROWS, LANES), F32)], 3,
    )(lines, response, tables["z"], tables["y"])[0]
    waves = call(middle_kernel, "middle", [VECTORS] * 4, [(2, XP * YP, LANES)], [], 2)(
        waves, tables["kernel"], tables["x"], tables["x_back"]
    )[0]
    return call(
        inverse_kernel, "inverse", [SCALARS, VECTORS, VECTORS, ANYWHERE, VECTORS, VECTORS], [(SENT_ROWS, LANES)],
        [pltpu.VMEM((LINE_ROWS, LANES), F32), pltpu.VMEM((FLAT_ROWS, LANES), F32), pltpu.VMEM((8, LANES), F32),
         pltpu.SemaphoreType.DMA], 3,
    )(signs, waves, lines, response, tables["y_back"], tables["z_back"])[0]


def per_device(ground_orbitals, occupation_signs, response_orbitals, window_offsets, ground_density):
    assert ground_orbitals.shape == (4, POINTS) and response_orbitals.shape[0] == 1
    basis_x, basis_y, basis_z = real_basis(NX), real_basis(NY), real_basis(NZ)
    tables = {
        "z": lane_table(basis_z.T), "z_back": lane_table(basis_z),
        "y": row_table(basis_y, YP), "y_back": row_table(basis_y.T, YP),
        "x": row_table(basis_x, XP), "x_back": row_table(basis_x.T, XP),
        "kernel": kernel_table(),
    }
    tables = {name: jnp.asarray(table) for name, table in tables.items()}
    flat = (SENT_ROWS, LANES)
    row = pltpu.VMEM((1, POINTS), F32)
    position = lax.axis_index("grid").reshape(1)
    term, own, kept, sent = call(
        prelude_kernel, "prelude", [SCALARS] * 3 + [ANYWHERE] * 2, [flat] * 4, [row, row, pltpu.SemaphoreType.DMA((2,))], 1
    )(position, occupation_signs, window_offsets, ground_orbitals, response_orbitals)
    count = lax.axis_size("orb")
    visiting = lax.ppermute(sent, "orb", [((i + 1) % count, i) for i in range(count)])
    density = summed_over_devices(term)
    lines = call(
        lines_kernel, "lines", [ANYWHERE], [(2, LINE_ROWS, LANES)],
        [pltpu.VMEM((4, 1, POINTS), F32), pltpu.VMEM((4, FLAT_ROWS, LANES), F32), pltpu.SemaphoreType.DMA((4,))], 2,
    )(ground_orbitals)[0]
    coefficient = call(coefficient_kernel, "coefficient", [VECTORS] * 2, [flat], [pltpu.VMEM(flat, F32)], 1)(
        ground_density.reshape(1, POINTS), own
    )[0]
    away = exchange_of(occupation_signs, lines, visiting, tables)
    second = lax.ppermute(away, "orb", [(i, (i + 1) % count) for i in range(count)])
    first = exchange_of(occupation_signs, lines, kept, tables)
    return call(finish_kernel, "finish", [VECTORS] * 4, [(1, POINTS)], [], 1)(coefficient, density, first, second)[0]


def solution(mesh):
    placed = (P("orb", None), P("orb"), P(("orb", "grid"), None), P(("orb", "grid"), None), P())
    return jax.shard_map(
        per_device, mesh=mesh, in_specs=placed, out_specs=P(("orb", "grid"), None), check_vma=False
    )
```

```python
import functools
import math

import numpy as np

import jax
import jax.numpy as jnp
from jax import lax
from jax.experimental import pallas as pl
from jax.experimental.pallas import tpu as pltpu
from jax.sharding import PartitionSpec as P

NX = 30
NY = 45
NZ = 60
SPACING = 0.5
SCREEN = 0.5
XC_COEF = 0.3282
HYBRID = 0.25

F32 = jnp.float32
BF16 = jnp.bfloat16
LANES = 128
POINTS = NX * NY * NZ
XP = 32
YP = 48
ZP = LANES // 2
LINES = math.lcm(NZ, LANES) // NZ
CHUNKS = math.lcm(NZ, LANES) // LANES
PERIODS = -(-NX * NY // LINES)
LINE_ROWS = PERIODS * LINES
FLAT_ROWS = PERIODS * CHUNKS
WHOLE = POINTS // LANES
TAIL = POINTS - WHOLE * LANES
SENT_ROWS = 640


def real_basis(count):
    waves = np.arange(count)
    folded = np.where(waves <= count // 2, waves, count - waves)
    angle = 2.0 * np.pi * np.outer(folded, waves) / count
    basis = np.where((waves <= count // 2)[:, None], np.cos(angle), np.sin(angle))
    return basis / np.sqrt(np.sum(basis**2, 1, keepdims=True))


def split_table(table):
    table = table.astype(np.float32)
    high = table.astype(jnp.bfloat16)
    return high, (table - high.astype(np.float32)).astype(jnp.bfloat16)


def padded(table, size):
    return np.pad(table, ((0, size - table.shape[0]), (0, size - table.shape[1])))


def lane_table(matrix):
    high, low = (np.kron(np.eye(2, dtype=jnp.bfloat16), padded(part, ZP)) for part in split_table(matrix))
    return np.block([[high, low], [high, np.zeros_like(low)]])


def row_table(matrix, size):
    high, low = (padded(part, size) for part in split_table(matrix))
    return np.concatenate([high, high, low], 1)


def kernel_table():
    def squares(count):
        places = np.arange(count)
        folded = np.where(places <= count // 2, places, places - count)
        waves = folded.astype(np.float32) * np.float32(2.0 * math.pi / (count * SPACING))
        return waves * waves

    squared = squares(NX)[None, :, None] + squares(NY)[:, None, None] + squares(NZ)[None, None, :]
    table = np.zeros((YP, XP, 2, ZP), np.float32)
    table[:NY, :NX, :, :NZ] = (4.0 * math.pi / (squared + SCREEN * SCREEN))[:, :, None, :]
    return table.reshape(YP * XP, LANES)


def split(values):
    high = values.astype(BF16)
    return high, (values - high.astype(F32)).astype(BF16)


def lane_product(values, table):
    high, low = split(values)
    halves = []
    for start in range(0, values.shape[1], LANES):
        lanes = slice(start, start + LANES)
        both = jnp.dot(jnp.concatenate([high[:, lanes], low[:, lanes]], 1), table, preferred_element_type=F32)
        halves.append(both[:, :LANES] + both[:, LANES:])
    return jnp.concatenate(halves, 1)


def row_product(table, values):
    high, low = split(values)
    return jnp.dot(table, jnp.concatenate([high, low, high], 0), preferred_element_type=F32)


def lane_ids(rows):
    return lax.broadcasted_iota(jnp.int32, (rows, LANES), 1)


def turned(values, shift):
    shift %= LANES
    return pltpu.roll(values, shift, 1) if shift else values


def line_of(flat, line, place):
    chunk, start = divmod(NZ * line, LANES)
    first = turned(flat[pl.ds(chunk, PERIODS, stride=CHUNKS), :], place - start)
    if start + NZ <= LANES:
        return first
    second = turned(flat[pl.ds(chunk + 1, PERIODS, stride=CHUNKS), :], place - start)
    return jnp.where(lane_ids(PERIODS) < place + LANES - start, first, second)


def to_lines(left, right, lines):
    ids = lane_ids(PERIODS)
    for line in range(LINES):
        low, high = line_of(left, line, 0), line_of(right, line, ZP)
        both = jnp.where(ids < NZ, low, jnp.where((ids >= ZP) & (ids < ZP + NZ), high, 0.0))
        lines[pl.ds(line, PERIODS, stride=LINES), :] = both


def to_flat(lines, flat):
    ids = lane_ids(PERIODS)
    for chunk in range(CHUNKS):
        low = chunk * LANES
        merged = None
        for line in range(low // NZ, -(-(low + LANES) // NZ)):
            value = turned(lines[pl.ds(line, PERIODS, stride=LINES), :], NZ * line - low)
            merged = value if merged is None else jnp.where(ids >= NZ * line - low, value, merged)
        flat[pl.ds(chunk, PERIODS, stride=CHUNKS), :] = merged


def fill_flat(row, flat):
    flat[pl.ds(0, WHOLE), :] = row.at[:, pl.ds(0, WHOLE * LANES)].reshape(WHOLE, LANES)[...]
    flat[pl.ds(WHOLE, flat.shape[0] - WHOLE), :] = jnp.zeros((flat.shape[0] - WHOLE, LANES), F32)
    flat[pl.ds(WHOLE, 1), pl.ds(0, TAIL)] = row[:, pl.ds(WHOLE * LANES, TAIL)]


def grouped(count, group, body):
    lax.fori_loop(0, count // group, lambda step, carry: (body(step * group), carry)[1], 0)


def prelude_kernel(position, signs, offsets, ground, response, term, own, kept, sent, row_g, row_r, sems):
    place = position[0]
    copies = [
        pltpu.make_async_copy(ground.at[pl.ds(place, 1), :], row_g, sems.at[0]),
        pltpu.make_async_copy(response, row_r, sems.at[1]),
    ]
    for copy in copies:
        copy.start()
    for copy in copies:
        copy.wait()
    fill_flat(row_g, own)
    fill_flat(row_r, kept)
    term[...] = signs[place].astype(F32) * own[...] * kept[...]
    sent[...] = kept[...]
    last = pl.ds(SENT_ROWS - 1, 1)
    kept[last, :] = jnp.full((1, LANES), offsets[0, 0].astype(F32))
    sent[last, :] = jnp.full((1, LANES), offsets[0, 1].astype(F32))


def lines_kernel(ground, lines, rows, flats, sems):
    copies = [
        pltpu.make_async_copy(ground.at[pl.ds(j, 1), :], rows.at[j], sems.at[j]) for j in range(4)
    ]
    for copy in copies:
        copy.start()
    for j in range(4):
        copies[j].wait()
        fill_flat(rows.at[j], flats.at[j])
    for half in range(2):
        to_lines(flats.at[2 * half], flats.at[2 * half + 1], lines.at[half])


def coefficient_kernel(density, own, coefficient, flat):
    fill_flat(density, flat)
    spots = lax.broadcasted_iota(jnp.int32, (SENT_ROWS, LANES), 0) * LANES + lane_ids(SENT_ROWS)
    values = jnp.where(spots < POINTS, flat[...], 1.0)
    coefficient[...] = -XC_COEF * jnp.exp(jnp.log(values) * (-2.0 / 3.0)) * own[...]


def solve_half(half, signs, lines, values, offset, tables, kernel, waves, turned_waves, total, prior):
    z_table, z_back, y_table, y_back, x_table, x_back = (table[...] for table in tables)
    group = 15
    for x in range(NX, XP):
        waves[pl.ds(x, YP, stride=XP), :] = jnp.zeros((YP, LANES), F32)
    for y in range(NY, YP):
        turned_waves[pl.ds(y, XP, stride=YP), :] = jnp.zeros((XP, LANES), F32)

    def forward(x):
        spots = [pl.ds((x + u) * NY, YP) for u in range(group)]
        value = lane_product(jnp.concatenate([lines[spot, :] * values[spot, :] for spot in spots], 0), z_table)
        value = row_product(y_table, jnp.concatenate([value[u * YP : (u + 1) * YP] for u in range(group)], 1))
        for u in range(group):
            waves[pl.ds(x + u, YP, stride=XP), :] = value[:, u * LANES : (u + 1) * LANES]

    def middle(y):
        spots = [pl.ds(pl.multiple_of((y + u) * XP, XP), XP) for u in range(group)]
        value = row_product(x_table, jnp.concatenate([waves[spot, :] for spot in spots], 1))
        value = row_product(x_back, value * jnp.concatenate([kernel[spot, :] for spot in spots], 1))
        for u in range(group):
            turned_waves[pl.ds(y + u, XP, stride=YP), :] = value[:, u * LANES : (u + 1) * LANES]

    ids = lane_ids(1)
    orbital = 2 * half + (ids >= ZP).astype(jnp.int32)
    sign = jnp.where(ids < ZP, signs[2 * half].astype(F32), signs[2 * half + 1].astype(F32))
    factor = jnp.where(orbital.astype(F32) >= offset, sign, 0.0)

    def backward(x):
        spots = [pl.ds(pl.multiple_of((x + u) * YP, YP), YP) for u in range(group)]
        value = row_product(y_back, jnp.concatenate([turned_waves[spot, :] for spot in spots], 1))
        value = jnp.concatenate([value[:, u * LANES : (u + 1) * LANES] for u in range(group)], 0)
        value = lane_product(value, z_back)
        for u in range(group):
            spot = pl.ds((x + u) * NY, YP)
            part = value[u * YP : (u + 1) * YP] * (lines[spot, :] * factor)
            if prior is not None:
                part += prior[spot, :]
                part += pltpu.roll(part, ZP, 1)
            total[spot, :] = part

    grouped(NX, group, forward)
    grouped(NY, group, middle)
    grouped(NX, group, backward)


def first_half_kernel(signs, lines, response, *refs):
    tables, (kernel, values, partial, flat, waves, turned_waves) = refs[:6], refs[6:]
    flat[pl.ds(0, WHOLE + 1), :] = response[pl.ds(0, WHOLE + 1), :]
    flat[pl.ds(WHOLE + 1, FLAT_ROWS - WHOLE - 1), :] = jnp.zeros((FLAT_ROWS - WHOLE - 1, LANES), F32)
    to_lines(flat, flat, values)
    offset = response[pl.ds(SENT_ROWS - 1, 1), :]
    solve_half(0, signs, lines.at[0], values, offset, tables, kernel, waves, turned_waves, partial, None)


def second_half_kernel(signs, lines, response, *refs):
    tables, (kernel, values, partial, exchange, flat, waves, turned_waves, total) = refs[:6], refs[6:]
    offset = response[pl.ds(SENT_ROWS - 1, 1), :]
    solve_half(1, signs, lines.at[1], values, offset, tables, kernel, waves, turned_waves, total, partial)
    to_flat(total, flat)
    exchange[...] = flat[pl.ds(0, SENT_ROWS), :]


def finish_kernel(coefficient, density, first, second, out):
    value = coefficient[...] * density[...] - HYBRID * (first[...] + second[...])
    out.at[:, pl.ds(0, WHOLE * LANES)].reshape(WHOLE, LANES)[...] = value[:WHOLE]
    out[:, pl.ds(WHOLE * LANES, TAIL)] = value[WHOLE : WHOLE + 1, :TAIL]


SCALARS = pl.BlockSpec(memory_space=pltpu.SMEM)
VECTORS = pl.BlockSpec(memory_space=pltpu.VMEM)
ANYWHERE = pl.BlockSpec(memory_space=pl.ANY)


def near(shape):
    return pltpu.VMEM(shape, F32) if shape != (1, POINTS) else jax.ShapeDtypeStruct(shape, F32)


def held(values):
    return pltpu.with_memory_space_constraint(values, pltpu.VMEM)


def call(body, name, specs, shapes, scratch, microseconds, outs=None):
    cost = pl.CostEstimate(flops=int(microseconds * 1e9), bytes_accessed=int(microseconds * 1e6), transcendentals=0)
    kernel = pl.pallas_call(
        body,
        name=name,
        in_specs=specs,
        out_shape=[near(shape) for shape in shapes],
        out_specs=[VECTORS] * len(shapes),
        scratch_shapes=scratch,
        cost_estimate=cost,
        compiler_params=pltpu.CompilerParams(vmem_limit_bytes=12 * 2**20),
    )
    return lambda *values: kernel(*(held(v) if spec is VECTORS else v for spec, v in zip(specs, values)))


def swap(values, axis, distance):
    count = lax.axis_size(axis)
    return lax.ppermute(values, axis, [(i, i ^ distance) for i in range(count)])


def summed_over_devices(term):
    orb_bits = [("orb", 1 << bit) for bit in range(lax.axis_size("orb").bit_length() - 1)]
    grid_bits = [("grid", 1 << bit) for bit in range(lax.axis_size("grid").bit_length() - 1)]
    split_bits, rest = orb_bits[:2], orb_bits[2:] + grid_bits
    for axis, distance in split_bits:
        bit = (lax.axis_index(axis) // distance) % 2
        pair = term.reshape(2, term.shape[0] // 2, LANES)
        kept = lax.dynamic_index_in_dim(pair, bit, 0, keepdims=False)
        sent = lax.dynamic_index_in_dim(pair, 1 - bit, 0, keepdims=False)
        term = kept + swap(sent, axis, distance)
    for axis, distance in rest:
        term = term + swap(term, axis, distance)
    for axis, distance in split_bits[::-1]:
        bit = (lax.axis_index(axis) // distance) % 2
        other = swap(term, axis, distance)
        term = jnp.concatenate([jnp.where(bit == 0, term, other), jnp.where(bit == 0, other, term)], 0)
    return term


def exchange_of(signs, lines, response, tables):
    shared = (signs, lines, response, *tables)
    flat, line = pltpu.VMEM((FLAT_ROWS, LANES), F32), pltpu.VMEM((LINE_ROWS, LANES), F32)
    waves = pltpu.VMEM((XP * YP, LANES), F32)
    specs = [SCALARS] + [VECTORS] * (2 + len(tables))
    values, partial = call(first_half_kernel, "first_half", specs, [(LINE_ROWS, LANES)] * 2, [flat, waves, waves], 3)(*shared)
    return call(
        second_half_kernel, "second_half", specs + [VECTORS] * 2, [(SENT_ROWS, LANES)], [flat, waves, waves, line], 3
    )(*shared, values, partial)[0]


def per_device(ground_orbitals, occupation_signs, response_orbitals, window_offsets, ground_density):
    assert ground_orbitals.shape == (4, POINTS) and response_orbitals.shape[0] == 1
    basis_x, basis_y, basis_z = real_basis(NX), real_basis(NY), real_basis(NZ)
    tables = (
        lane_table(basis_z.T), lane_table(basis_z),
        row_table(basis_y, YP), row_table(basis_y.T, YP),
        row_table(basis_x, XP), row_table(basis_x.T, XP),
        kernel_table(),
    )
    tables = tuple(jnp.asarray(table) for table in tables)
    flat = (SENT_ROWS, LANES)
    row = pltpu.VMEM((1, POINTS), F32)
    position = lax.axis_index("grid").reshape(1)
    term, own, kept, sent = call(
        prelude_kernel, "prelude", [SCALARS] * 3 + [ANYWHERE] * 2, [flat] * 4, [row, row, pltpu.SemaphoreType.DMA((2,))], 1
    )(position, occupation_signs, window_offsets, ground_orbitals, response_orbitals)
    count = lax.axis_size("orb")
    visiting = lax.ppermute(sent, "orb", [((i + 1) % count, i) for i in range(count)])
    density = summed_over_devices(term)
    lines = call(
        lines_kernel, "lines", [ANYWHERE], [(2, LINE_ROWS, LANES)],
        [pltpu.VMEM((4, 1, POINTS), F32), pltpu.VMEM((4, FLAT_ROWS, LANES), F32), pltpu.SemaphoreType.DMA((4,))], 2,
    )(ground_orbitals)[0]
    coefficient = call(coefficient_kernel, "coefficient", [VECTORS] * 2, [flat], [pltpu.VMEM(flat, F32)], 1)(
        ground_density.reshape(1, POINTS), own
    )[0]
    away = exchange_of(occupation_signs, lines, visiting, tables)
    second = lax.ppermute(away, "orb", [(i, (i + 1) % count) for i in range(count)])
    first = exchange_of(occupation_signs, lines, kept, tables)
    return call(finish_kernel, "finish", [VECTORS] * 4, [(1, POINTS)], [], 1)(coefficient, density, first, second)[0]


def solution(mesh):
    placed = (P("orb", None), P("orb"), P(("orb", "grid"), None), P(("orb", "grid"), None), P())
    return jax.shard_map(
        per_device, mesh=mesh, in_specs=placed, out_specs=P(("orb", "grid"), None), check_vma=False
    )
```

```python
import functools
import math

import numpy as np

import jax
import jax.numpy as jnp
from jax import lax
from jax.experimental import pallas as pl
from jax.experimental.pallas import tpu as pltpu
from jax.sharding import PartitionSpec as P

NX = 30
NY = 45
NZ = 60
SPACING = 0.5
SCREEN = 0.5
XC_COEF = 0.3282
HYBRID = 0.25

F32 = jnp.float32
BF16 = jnp.bfloat16
LANES = 128
POINTS = NX * NY * NZ
XP = 32
YP = 48
ZP = LANES // 2
XS = XP + 1
YS = YP + 1
LINES = math.lcm(NZ, LANES) // NZ
CHUNKS = math.lcm(NZ, LANES) // LANES
PERIODS = -(-NX * NY // LINES)
LINE_ROWS = PERIODS * LINES
FLAT_ROWS = PERIODS * CHUNKS
WHOLE = POINTS // LANES
TAIL = POINTS - WHOLE * LANES
SENT_ROWS = 640


def real_basis(count):
    waves = np.arange(count)
    folded = np.where(waves <= count // 2, waves, count - waves)
    angle = 2.0 * np.pi * np.outer(folded, waves) / count
    basis = np.where((waves <= count // 2)[:, None], np.cos(angle), np.sin(angle))
    return basis / np.sqrt(np.sum(basis**2, 1, keepdims=True))


def split_table(table):
    table = table.astype(np.float32)
    high = table.astype(jnp.bfloat16)
    return high, (table - high.astype(np.float32)).astype(jnp.bfloat16)


def padded(table, size):
    return np.pad(table, ((0, size - table.shape[0]), (0, size - table.shape[1])))


def lane_table(matrix):
    high, low = (np.kron(np.eye(2, dtype=jnp.bfloat16), padded(part, ZP)) for part in split_table(matrix))
    return np.block([[high, low], [high, np.zeros_like(low)]])


def row_table(matrix, size):
    high, low = (padded(part, size) for part in split_table(matrix))
    return np.concatenate([high, high, low], 1)


def kernel_table():
    def squares(count):
        places = np.arange(count)
        folded = np.where(places <= count // 2, places, places - count)
        waves = folded.astype(np.float32) * np.float32(2.0 * math.pi / (count * SPACING))
        return waves * waves

    squared = squares(NX)[None, :, None] + squares(NY)[:, None, None] + squares(NZ)[None, None, :]
    table = np.zeros((YP, XP, 2, ZP), np.float32)
    table[:NY, :NX, :, :NZ] = (4.0 * math.pi / (squared + SCREEN * SCREEN))[:, :, None, :]
    return table.reshape(YP * XP, LANES)


def split(values):
    high = values.astype(BF16)
    return high, (values - high.astype(F32)).astype(BF16)


def lane_product(values, table):
    high, low = split(values)
    halves = []
    for start in range(0, values.shape[1], LANES):
        lanes = slice(start, start + LANES)
        both = jnp.dot(jnp.concatenate([high[:, lanes], low[:, lanes]], 1), table, preferred_element_type=F32)
        halves.append(both[:, :LANES] + both[:, LANES:])
    return jnp.concatenate(halves, 1)


def row_product(table, values):
    high, low = split(values)
    return jnp.dot(table, jnp.concatenate([high, low, high], 0), preferred_element_type=F32)


def lane_ids(rows):
    return lax.broadcasted_iota(jnp.int32, (rows, LANES), 1)


def turned(values, shift):
    shift %= LANES
    return pltpu.roll(values, shift, 1) if shift else values


def line_of(flat, line, place):
    chunk, start = divmod(NZ * line, LANES)
    first = turned(flat[pl.ds(chunk, PERIODS, stride=CHUNKS), :], place - start)
    if start + NZ <= LANES:
        return first
    second = turned(flat[pl.ds(chunk + 1, PERIODS, stride=CHUNKS), :], place - start)
    return jnp.where(lane_ids(PERIODS) < place + LANES - start, first, second)


def to_lines(left, right, lines, pitched):
    ids = lane_ids(PERIODS)
    for line in range(LINES):
        low, high = line_of(left, line, 0), line_of(right, line, ZP)
        both = jnp.where(ids < NZ, low, jnp.where((ids >= ZP) & (ids < ZP + NZ), high, 0.0))
        pitched[pl.ds(line, PERIODS, stride=LINES + 1), :] = both
    for period in range(PERIODS):
        lines[pl.ds(period * LINES, LINES), :] = pitched[pl.ds(period * (LINES + 1), LINES), :]


def to_flat(lines, flat, pitched):
    ids = lane_ids(PERIODS)
    for period in range(PERIODS):
        pitched[pl.ds(period * (LINES + 1), LINES), :] = lines[pl.ds(period * LINES, LINES), :]
    for chunk in range(CHUNKS):
        low = chunk * LANES
        merged = None
        for line in range(low // NZ, -(-(low + LANES) // NZ)):
            value = turned(pitched[pl.ds(line, PERIODS, stride=LINES + 1), :], NZ * line - low)
            merged = value if merged is None else jnp.where(ids >= NZ * line - low, value, merged)
        flat[pl.ds(chunk, PERIODS, stride=CHUNKS), :] = merged


def body_copy(row, flat, sem):
    target = flat.at[pl.ds(0, WHOLE), :].reshape(1, WHOLE * LANES)
    return pltpu.make_async_copy(row.at[:, pl.ds(0, WHOLE * LANES)], target, sem)


def fill_tail(tail, flat):
    flat[pl.ds(WHOLE, flat.shape[0] - WHOLE), :] = jnp.zeros((flat.shape[0] - WHOLE, LANES), F32)
    flat[pl.ds(WHOLE, 1), pl.ds(0, TAIL)] = tail


def grouped(count, group, body):
    lax.fori_loop(0, count // group, lambda step, carry: (body(step * group), carry)[1], 0)


def prelude_kernel(position, signs, offsets, ground, response, term, own, kept, weights, rows, sign, offset, sems):
    place = position[0]
    spot = pl.ds(place, 1)
    copies = [
        pltpu.make_async_copy(signs, sign, sems.at[0]),
        pltpu.make_async_copy(offsets, offset, sems.at[1]),
        body_copy(response, kept, sems.at[2]),
        pltpu.make_async_copy(response, rows.at[0], sems.at[3]),
        body_copy(ground.at[spot, :], own, sems.at[4]),
        pltpu.make_async_copy(ground.at[spot, :], rows.at[1], sems.at[5]),
    ]
    for copy in copies:
        copy.start()
    for copy in copies:
        copy.wait()
    last = pl.ds(WHOLE * LANES, TAIL)
    fill_tail(rows[0, :, last], kept)
    fill_tail(rows[1, :, last], own)
    term[...] = sign[place].astype(F32) * own[...] * kept[...]
    for step in range(2):
        kept[pl.ds(SENT_ROWS - 2 + step, 1), :] = jnp.full((1, LANES), offset[0, step].astype(F32))
    ids = lane_ids(1)
    for half in range(2):
        pair = jnp.where(ids < ZP, sign[2 * half].astype(F32), sign[2 * half + 1].astype(F32))
        weights[pl.ds(half, 1), :] = pair


def lines_kernel(ground, low_lines, high_lines, flats, pitched, sems):
    copies = [body_copy(ground.at[pl.ds(j, 1), :], flats.at[j], sems.at[j]) for j in range(4)]
    for copy in copies:
        copy.start()
    for j in range(4):
        copies[j].wait()
        fill_tail(ground[pl.ds(j, 1), pl.ds(WHOLE * LANES, TAIL)], flats.at[j])
    to_lines(flats.at[0], flats.at[1], low_lines, pitched)
    to_lines(flats.at[2], flats.at[3], high_lines, pitched)


def coefficient_kernel(density, own, coefficient, values, sem):
    copy = pltpu.make_async_copy(density, values, sem)
    copy.start()
    copy.wait()
    block = 8 * LANES
    for start in range(0, POINTS, block):
        size = min(block, POINTS - start)
        shape = (8, LANES) if size == block else (1, size)
        value = values[pl.ds(start, size)].reshape(shape)
        value = -XC_COEF * jnp.exp(jnp.log(value) * (-2.0 / 3.0))
        spot = (pl.ds(start // LANES, shape[0]), pl.ds(0, shape[1]))
        coefficient[spot] = value * own[spot]


def solve_half(half, step, weights, lines, values, response, tables, kernel_copy, scratch, total, prior):
    kernel, waves, turned_waves = scratch
    z_table, z_back, y_table, y_back, x_table, x_back = (table[...] for table in tables)
    group = 15
    for x in range(NX, XP):
        waves[pl.ds(x, YP, stride=XS), :] = jnp.zeros((YP, LANES), F32)
    for y in range(NY, YP):
        turned_waves[pl.ds(y, XP, stride=YS), :] = jnp.zeros((XP, LANES), F32)

    def forward(x):
        spots = [pl.ds((x + u) * NY, YP) for u in range(group)]
        value = lane_product(jnp.concatenate([lines[spot, :] * values[spot, :] for spot in spots], 0), z_table)
        value = row_product(y_table, jnp.concatenate([value[u * YP : (u + 1) * YP] for u in range(group)], 1))
        for u in range(group):
            waves[pl.ds(x + u, YP, stride=XS), :] = value[:, u * LANES : (u + 1) * LANES]

    def middle(y):
        spots = [pl.ds(pl.multiple_of((y + u) * XP, XP), XP) for u in range(group)]
        value = row_product(x_table, jnp.concatenate([waves[pl.ds((y + u) * XS, XP), :] for u in range(group)], 1))
        value = row_product(x_back, value * jnp.concatenate([kernel[spot, :] for spot in spots], 1))
        for u in range(group):
            turned_waves[pl.ds(y + u, XP, stride=YS), :] = value[:, u * LANES : (u + 1) * LANES]

    orbital = 2 * half + (lane_ids(1) >= ZP).astype(jnp.int32)
    offset = response[pl.ds(SENT_ROWS - 2 + step, 1), :]
    factor = jnp.where(orbital.astype(F32) >= offset, weights[pl.ds(half, 1), :], 0.0)

    def backward(x):
        spots = [pl.ds((x + u) * YS, YP) for u in range(group)]
        value = row_product(y_back, jnp.concatenate([turned_waves[spot, :] for spot in spots], 1))
        value = jnp.concatenate([value[:, u * LANES : (u + 1) * LANES] for u in range(group)], 0)
        value = lane_product(value, z_back)
        for u in range(group):
            spot = pl.ds((x + u) * NY, YP)
            part = value[u * YP : (u + 1) * YP] * (lines[spot, :] * factor)
            if prior is not None:
                part += prior[spot, :]
                part += pltpu.roll(part, ZP, 1)
            total[spot, :] = part

    grouped(NX, group, forward)
    kernel_copy.wait()
    grouped(NY, group, middle)
    grouped(NX, group, backward)


def first_half_kernel(step, weights, lines, response, *refs):
    tables, (kernel, values, partial, flat, pitched, sem, *scratch) = refs[:6], refs[6:]
    kernel_copy = pltpu.make_async_copy(kernel, scratch[0], sem)
    kernel_copy.start()
    flat[pl.ds(0, WHOLE + 1), :] = response[pl.ds(0, WHOLE + 1), :]
    flat[pl.ds(WHOLE + 1, FLAT_ROWS - WHOLE - 1), :] = jnp.zeros((FLAT_ROWS - WHOLE - 1, LANES), F32)
    to_lines(flat, flat, values, pitched)
    solve_half(0, step, weights, lines, values, response, tables, kernel_copy, scratch, partial, None)


def second_half_kernel(step, weights, lines, response, *refs):
    tables, (kernel, values, partial, exchange, flat, pitched, sem, *scratch, total) = refs[:6], refs[6:]
    kernel_copy = pltpu.make_async_copy(kernel, scratch[0], sem)
    kernel_copy.start()
    solve_half(1, step, weights, lines, values, response, tables, kernel_copy, scratch, total, partial)
    to_flat(total, flat, pitched)
    exchange[...] = flat[pl.ds(0, SENT_ROWS), :]


def finish_kernel(coefficient, density, first, second, out):
    value = coefficient[...] * density[...] - HYBRID * (first[...] + second[...])
    out.at[:, pl.ds(0, WHOLE * LANES)].reshape(WHOLE, LANES)[...] = value[:WHOLE]
    out[:, pl.ds(WHOLE * LANES, TAIL)] = value[WHOLE : WHOLE + 1, :TAIL]


SCALARS = pl.BlockSpec(memory_space=pltpu.SMEM)
VECTORS = pl.BlockSpec(memory_space=pltpu.VMEM)
FAR = pl.BlockSpec(memory_space=pltpu.HBM)


def near(shape):
    return pltpu.VMEM(shape, F32) if shape != (1, POINTS) else jax.ShapeDtypeStruct(shape, F32)


def placed(values, spec):
    space = {id(FAR): pltpu.HBM, id(VECTORS): pltpu.VMEM}.get(id(spec))
    return values if space is None else pltpu.with_memory_space_constraint(values, space)


def call(body, name, specs, shapes, scratch, microseconds, outs=None):
    cost = pl.CostEstimate(flops=int(microseconds * 1e9), bytes_accessed=int(microseconds * 1e6), transcendentals=0)
    kernel = pl.pallas_call(
        body,
        name=name,
        in_specs=specs,
        out_shape=[near(shape) for shape in shapes],
        out_specs=[VECTORS] * len(shapes),
        scratch_shapes=scratch,
        cost_estimate=cost,
        compiler_params=pltpu.CompilerParams(vmem_limit_bytes=12 * 2**20),
    )
    return lambda *values: kernel(*(placed(v, spec) for spec, v in zip(specs, values)))


def swap(values, axis, distance):
    count = lax.axis_size(axis)
    return lax.ppermute(values, axis, [(i, i ^ distance) for i in range(count)])


def summed_over_devices(term):
    orb_bits = [("orb", 1 << bit) for bit in range(lax.axis_size("orb").bit_length() - 1)]
    grid_bits = [("grid", 1 << bit) for bit in range(lax.axis_size("grid").bit_length() - 1)]
    split_bits, rest = orb_bits[:2], orb_bits[2:] + grid_bits
    for axis, distance in split_bits:
        bit = (lax.axis_index(axis) // distance) % 2
        pair = term.reshape(2, term.shape[0] // 2, LANES)
        kept = lax.dynamic_index_in_dim(pair, bit, 0, keepdims=False)
        sent = lax.dynamic_index_in_dim(pair, 1 - bit, 0, keepdims=False)
        term = kept + swap(sent, axis, distance)
    for axis, distance in rest:
        term = term + swap(term, axis, distance)
    for axis, distance in split_bits[::-1]:
        bit = (lax.axis_index(axis) // distance) % 2
        other = swap(term, axis, distance)
        term = jnp.concatenate([jnp.where(bit == 0, term, other), jnp.where(bit == 0, other, term)], 0)
    return term


def half_call(body, name, step, shapes, extra, values):
    flat, pitched = pltpu.VMEM((FLAT_ROWS, LANES), F32), pltpu.VMEM((PERIODS * (LINES + 1), LANES), F32)
    scratch = [flat, pitched, pltpu.SemaphoreType.DMA, pltpu.VMEM((YP * XP, LANES), F32)]
    scratch += [pltpu.VMEM((YP * XS, LANES), F32), pltpu.VMEM((XP * YS, LANES), F32)] + extra
    specs = [VECTORS] * 9 + [FAR] + [VECTORS] * (len(values) - 10)
    return call(functools.partial(body, step), name, specs, shapes, scratch, 3)(*values)


def first_half(step, *shared):
    return half_call(first_half_kernel, "first_half", step, [(LINE_ROWS, LANES)] * 2, [], shared)


def second_half(step, *shared):
    line = pltpu.VMEM((LINE_ROWS, LANES), F32)
    return half_call(second_half_kernel, "second_half", step, [(SENT_ROWS, LANES)], [line], shared)[0]


def per_device(ground_orbitals, occupation_signs, response_orbitals, window_offsets, ground_density):
    assert ground_orbitals.shape == (4, POINTS) and response_orbitals.shape[0] == 1
    basis_x, basis_y, basis_z = real_basis(NX), real_basis(NY), real_basis(NZ)
    tables = (
        lane_table(basis_z.T), lane_table(basis_z),
        row_table(basis_y, YP), row_table(basis_y.T, YP),
        row_table(basis_x, XP), row_table(basis_x.T, XP),
        kernel_table(),
    )
    tables = tuple(jnp.asarray(table) for table in tables)
    flat = (SENT_ROWS, LANES)
    position = lax.axis_index("grid").reshape(1)
    scratch = [pltpu.VMEM((2, 1, POINTS), F32), pltpu.SMEM((4,), jnp.int32), pltpu.SMEM((1, 2), jnp.int32)]
    term, own, kept, weights = call(
        prelude_kernel, "prelude", [SCALARS] + [FAR] * 4, [flat] * 3 + [(8, LANES)],
        scratch + [pltpu.SemaphoreType.DMA((6,))], 1,
    )(position, occupation_signs, window_offsets, ground_orbitals, response_orbitals)
    count = lax.axis_size("orb")
    visiting = lax.ppermute(kept, "orb", [((i + 1) % count, i) for i in range(count)])
    density = summed_over_devices(term)
    low_lines, high_lines = call(
        lines_kernel, "lines", [VECTORS], [(LINE_ROWS, LANES)] * 2,
        [pltpu.VMEM((4, FLAT_ROWS, LANES), F32), pltpu.VMEM((PERIODS * (LINES + 1), LANES), F32),
         pltpu.SemaphoreType.DMA((4,))], 2,
    )(ground_orbitals)
    coefficient = call(
        coefficient_kernel, "coefficient", [FAR, VECTORS], [flat],
        [pltpu.VMEM((POINTS,), F32), pltpu.SemaphoreType.DMA], 1,
    )(ground_density, own)[0]
    values, partial = first_half(0, weights, low_lines, kept, *tables)
    away_values, away_partial = first_half(1, weights, low_lines, visiting, *tables)
    away = second_half(1, weights, high_lines, visiting, *tables, away_values, away_partial)
    second = lax.ppermute(away, "orb", [(i, (i + 1) % count) for i in range(count)])
    values, away = lax.optimization_barrier((values, away))
    first = second_half(0, weights, high_lines, kept, *tables, values, partial)
    return call(finish_kernel, "finish", [VECTORS] * 4, [(1, POINTS)], [], 1)(coefficient, density, first, second)[0]


def solution(mesh):
    placed = (P("orb", None), P("orb"), P(("orb", "grid"), None), P(("orb", "grid"), None), P())
    return jax.shard_map(
        per_device, mesh=mesh, in_specs=placed, out_specs=P(("orb", "grid"), None), check_vma=False
    )
```

```python
import functools
import math

import numpy as np

import jax
import jax.numpy as jnp
from jax import lax
from jax.experimental import pallas as pl
from jax.experimental.pallas import tpu as pltpu
from jax.sharding import PartitionSpec as P

NX = 30
NY = 45
NZ = 60
SPACING = 0.5
SCREEN = 0.5
XC_COEF = 0.3282
HYBRID = 0.25

F32 = jnp.float32
BF16 = jnp.bfloat16
LANES = 128
POINTS = NX * NY * NZ
XP = 32
YP = 48
ZP = LANES // 2
XS = XP + 1
YS = YP + 1
LINES = math.lcm(NZ, LANES) // NZ
CHUNKS = math.lcm(NZ, LANES) // LANES
PERIODS = -(-NX * NY // LINES)
LINE_ROWS = PERIODS * LINES
FLAT_ROWS = PERIODS * CHUNKS
WHOLE = POINTS // LANES
TAIL = POINTS - WHOLE * LANES
SENT_ROWS = 640


def real_basis(count):
    waves = np.arange(count)
    folded = np.where(waves <= count // 2, waves, count - waves)
    angle = 2.0 * np.pi * np.outer(folded, waves) / count
    basis = np.where((waves <= count // 2)[:, None], np.cos(angle), np.sin(angle))
    return basis / np.sqrt(np.sum(basis**2, 1, keepdims=True))


def split_table(table):
    table = table.astype(np.float32)
    high = table.astype(jnp.bfloat16)
    return high, (table - high.astype(np.float32)).astype(jnp.bfloat16)


def padded(table, size):
    return np.pad(table, ((0, size - table.shape[0]), (0, size - table.shape[1])))


def lane_table(matrix):
    high, low = (np.kron(np.eye(2, dtype=jnp.bfloat16), padded(part, ZP)) for part in split_table(matrix))
    return np.block([[high, low], [high, np.zeros_like(low)]])


def row_table(matrix, size):
    high, low = (padded(part, size) for part in split_table(matrix))
    return np.concatenate([high, high, low], 1)


def kernel_table():
    def squares(count):
        places = np.arange(count)
        folded = np.where(places <= count // 2, places, places - count)
        waves = folded.astype(np.float32) * np.float32(2.0 * math.pi / (count * SPACING))
        return waves * waves

    squared = squares(NX)[None, :, None] + squares(NY)[:, None, None] + squares(NZ)[None, None, :]
    table = np.zeros((YP, XP, 2, ZP), np.float32)
    table[:NY, :NX, :, :NZ] = (4.0 * math.pi / (squared + SCREEN * SCREEN))[:, :, None, :]
    return table.reshape(YP * XP, LANES)


def split(values):
    high = values.astype(BF16)
    return high, (values - high.astype(F32)).astype(BF16)


def lane_product(values, table):
    high, low = split(values)
    halves = []
    for start in range(0, values.shape[1], LANES):
        lanes = slice(start, start + LANES)
        both = jnp.dot(jnp.concatenate([high[:, lanes], low[:, lanes]], 1), table, preferred_element_type=F32)
        halves.append(both[:, :LANES] + both[:, LANES:])
    return jnp.concatenate(halves, 1)


def row_product(table, values):
    high, low = split(values)
    return jnp.dot(table, jnp.concatenate([high, low, high], 0), preferred_element_type=F32)


def lane_ids(rows):
    return lax.broadcasted_iota(jnp.int32, (rows, LANES), 1)


def turned(values, shift):
    shift %= LANES
    return pltpu.roll(values, shift, 1) if shift else values


def line_of(flat, line, place):
    chunk, start = divmod(NZ * line, LANES)
    first = turned(flat[pl.ds(chunk, PERIODS, stride=CHUNKS), :], place - start)
    if start + NZ <= LANES:
        return first
    second = turned(flat[pl.ds(chunk + 1, PERIODS, stride=CHUNKS), :], place - start)
    return jnp.where(lane_ids(PERIODS) < place + LANES - start, first, second)


def to_lines(left, right, lines, pitched):
    ids = lane_ids(PERIODS)
    for line in range(LINES):
        low, high = line_of(left, line, 0), line_of(right, line, ZP)
        both = jnp.where(ids < NZ, low, jnp.where((ids >= ZP) & (ids < ZP + NZ), high, 0.0))
        pitched[pl.ds(line, PERIODS, stride=LINES + 1), :] = both
    for period in range(PERIODS):
        lines[pl.ds(period * LINES, LINES), :] = pitched[pl.ds(period * (LINES + 1), LINES), :]


def to_flat(lines, flat, pitched):
    ids = lane_ids(PERIODS)
    for period in range(PERIODS):
        pitched[pl.ds(period * (LINES + 1), LINES), :] = lines[pl.ds(period * LINES, LINES), :]
    for chunk in range(CHUNKS):
        low = chunk * LANES
        merged = None
        for line in range(low // NZ, -(-(low + LANES) // NZ)):
            value = turned(pitched[pl.ds(line, PERIODS, stride=LINES + 1), :], NZ * line - low)
            merged = value if merged is None else jnp.where(ids >= NZ * line - low, value, merged)
        flat[pl.ds(chunk, PERIODS, stride=CHUNKS), :] = merged


def body_copy(row, flat, sem):
    target = flat.at[pl.ds(0, WHOLE), :].reshape(1, WHOLE * LANES)
    return pltpu.make_async_copy(row.at[:, pl.ds(0, WHOLE * LANES)], target, sem)


def fill_tail(tail, flat):
    flat[pl.ds(WHOLE, flat.shape[0] - WHOLE), :] = jnp.zeros((flat.shape[0] - WHOLE, LANES), F32)
    flat[pl.ds(WHOLE, 1), pl.ds(0, TAIL)] = tail


def grouped(count, group, body):
    lax.fori_loop(0, count // group, lambda step, carry: (body(step * group), carry)[1], 0)


def prelude_kernel(signs, offsets, ground, response, stays, goes, own, kept, weights, rows, sign, offset, term, sems):
    place = lax.axis_index("grid")
    spot = pl.ds(place, 1)
    copies = [
        pltpu.make_async_copy(signs, sign, sems.at[0]),
        pltpu.make_async_copy(offsets, offset, sems.at[1]),
        body_copy(response, kept, sems.at[2]),
        pltpu.make_async_copy(response, rows.at[0], sems.at[3]),
        body_copy(ground.at[spot, :], own, sems.at[4]),
        pltpu.make_async_copy(ground.at[spot, :], rows.at[1], sems.at[5]),
    ]
    for copy in copies:
        copy.start()
    for copy in copies:
        copy.wait()
    last = pl.ds(WHOLE * LANES, TAIL)
    fill_tail(rows[0, :, last], kept)
    fill_tail(rows[1, :, last], own)
    term[...] = sign[place].astype(F32) * own[...] * kept[...]
    share(term, 1, stays, goes)
    for step in range(2):
        kept[pl.ds(SENT_ROWS - 2 + step, 1), :] = jnp.full((1, LANES), offset[0, step].astype(F32))
    ids = lane_ids(1)
    for half in range(2):
        pair = jnp.where(ids < ZP, sign[2 * half].astype(F32), sign[2 * half + 1].astype(F32))
        weights[pl.ds(half, 1), :] = pair


def lines_kernel(ground, low_lines, high_lines, flats, pitched, sems):
    copies = [body_copy(ground.at[pl.ds(j, 1), :], flats.at[j], sems.at[j]) for j in range(4)]
    for copy in copies:
        copy.start()
    for j in range(4):
        copies[j].wait()
        fill_tail(ground[pl.ds(j, 1), pl.ds(WHOLE * LANES, TAIL)], flats.at[j])
    to_lines(flats.at[0], flats.at[1], low_lines, pitched)
    to_lines(flats.at[2], flats.at[3], high_lines, pitched)


def coefficient_kernel(density, own, coefficient, values, sem):
    copy = pltpu.make_async_copy(density, values, sem)
    copy.start()
    copy.wait()
    block = 8 * LANES
    for start in range(0, POINTS, block):
        size = min(block, POINTS - start)
        shape = (8, LANES) if size == block else (1, size)
        value = values[pl.ds(start, size)].reshape(shape)
        value = -XC_COEF * jnp.exp(jnp.log(value) * (-2.0 / 3.0))
        spot = (pl.ds(start // LANES, shape[0]), pl.ds(0, shape[1]))
        coefficient[spot] = value * own[spot]


def solve_half(half, step, weights, lines, values, response, tables, kernel_copy, scratch, total, prior):
    kernel, waves, turned_waves = scratch
    z_table, z_back, y_table, y_back, x_table, x_back = (table[...] for table in tables)
    group = 15
    for x in range(NX, XP):
        waves[pl.ds(x, YP, stride=XS), :] = jnp.zeros((YP, LANES), F32)
    for y in range(NY, YP):
        turned_waves[pl.ds(y, XP, stride=YS), :] = jnp.zeros((XP, LANES), F32)

    def forward(x):
        spots = [pl.ds((x + u) * NY, YP) for u in range(group)]
        value = lane_product(jnp.concatenate([lines[spot, :] * values[spot, :] for spot in spots], 0), z_table)
        value = row_product(y_table, jnp.concatenate([value[u * YP : (u + 1) * YP] for u in range(group)], 1))
        for u in range(group):
            waves[pl.ds(x + u, YP, stride=XS), :] = value[:, u * LANES : (u + 1) * LANES]

    def middle(y):
        spots = [pl.ds(pl.multiple_of((y + u) * XP, XP), XP) for u in range(group)]
        value = row_product(x_table, jnp.concatenate([waves[pl.ds((y + u) * XS, XP), :] for u in range(group)], 1))
        value = row_product(x_back, value * jnp.concatenate([kernel[spot, :] for spot in spots], 1))
        for u in range(group):
            turned_waves[pl.ds(y + u, XP, stride=YS), :] = value[:, u * LANES : (u + 1) * LANES]

    orbital = 2 * half + (lane_ids(1) >= ZP).astype(jnp.int32)
    offset = response[pl.ds(SENT_ROWS - 2 + step, 1), :]
    factor = jnp.where(orbital.astype(F32) >= offset, weights[pl.ds(half, 1), :], 0.0)

    def backward(x):
        spots = [pl.ds((x + u) * YS, YP) for u in range(group)]
        value = row_product(y_back, jnp.concatenate([turned_waves[spot, :] for spot in spots], 1))
        value = jnp.concatenate([value[:, u * LANES : (u + 1) * LANES] for u in range(group)], 0)
        value = lane_product(value, z_back)
        for u in range(group):
            spot = pl.ds((x + u) * NY, YP)
            part = value[u * YP : (u + 1) * YP] * (lines[spot, :] * factor)
            if prior is not None:
                part += prior[spot, :]
                part += pltpu.roll(part, ZP, 1)
            total[spot, :] = part

    grouped(NX, group, forward)
    kernel_copy.wait()
    grouped(NY, group, middle)
    grouped(NX, group, backward)


def first_half_kernel(step, weights, lines, response, *refs):
    tables, (kernel, values, partial, flat, pitched, sem, *scratch) = refs[:6], refs[6:]
    kernel_copy = pltpu.make_async_copy(kernel, scratch[0], sem)
    kernel_copy.start()
    flat[pl.ds(0, WHOLE + 1), :] = response[pl.ds(0, WHOLE + 1), :]
    flat[pl.ds(WHOLE + 1, FLAT_ROWS - WHOLE - 1), :] = jnp.zeros((FLAT_ROWS - WHOLE - 1, LANES), F32)
    to_lines(flat, flat, values, pitched)
    solve_half(0, step, weights, lines, values, response, tables, kernel_copy, scratch, partial, None)


def second_half_kernel(step, weights, lines, response, *refs):
    tables, (kernel, values, partial, exchange, flat, pitched, sem, *scratch, total) = refs[:6], refs[6:]
    kernel_copy = pltpu.make_async_copy(kernel, scratch[0], sem)
    kernel_copy.start()
    solve_half(1, step, weights, lines, values, response, tables, kernel_copy, scratch, total, partial)
    to_flat(total, flat, pitched)
    exchange[...] = flat[pl.ds(0, SENT_ROWS), :]


def finish_kernel(coefficient, mine, other, first, second, out, density):
    join_kernel(1, mine, other, density)
    value = coefficient[...] * density[...] - HYBRID * (first[...] + second[...])
    out.at[:, pl.ds(0, WHOLE * LANES)].reshape(WHOLE, LANES)[...] = value[:WHOLE]
    out[:, pl.ds(WHOLE * LANES, TAIL)] = value[WHOLE : WHOLE + 1, :TAIL]


SCALARS = pl.BlockSpec(memory_space=pltpu.SMEM)
VECTORS = pl.BlockSpec(memory_space=pltpu.VMEM)
FAR = pl.BlockSpec(memory_space=pltpu.HBM)


def near(shape):
    return pltpu.VMEM(shape, F32) if shape != (1, POINTS) else jax.ShapeDtypeStruct(shape, F32)


def placed(values, spec):
    space = {id(FAR): pltpu.HBM, id(VECTORS): pltpu.VMEM}.get(id(spec))
    return values if space is None else pltpu.with_memory_space_constraint(values, space)


def call(body, name, specs, shapes, scratch, microseconds, outs=None):
    cost = pl.CostEstimate(flops=int(microseconds * 1e9), bytes_accessed=int(microseconds * 1e6), transcendentals=0)
    kernel = pl.pallas_call(
        body,
        name=name,
        in_specs=specs,
        out_shape=[near(shape) for shape in shapes],
        out_specs=[VECTORS] * len(shapes),
        scratch_shapes=scratch,
        cost_estimate=cost,
        compiler_params=pltpu.CompilerParams(vmem_limit_bytes=12 * 2**20),
    )
    return lambda *values: kernel(*(placed(v, spec) for spec, v in zip(specs, values)))


def orb_bit(distance):
    return lax.rem(lax.div(lax.axis_index("orb"), distance), 2)


def share(term, distance, stays, goes):
    half, bit = stays.shape[0], orb_bit(distance)
    stays[...] = term[pl.ds(pl.multiple_of(bit * half, half), half), :]
    goes[...] = term[pl.ds(pl.multiple_of((1 - bit) * half, half), half), :]


def share_kernel(distance, mine, other, stays, goes, term):
    term[...] = mine[...] + other[...]
    share(term, distance, stays, goes)


def add_kernel(mine, other, out):
    out[...] = mine[...] + other[...]


def join_kernel(distance, mine, other, out):
    half, bit = mine.shape[0], orb_bit(distance)
    out[pl.ds(pl.multiple_of(bit * half, half), half), :] = mine[...]
    out[pl.ds(pl.multiple_of((1 - bit) * half, half), half), :] = other[...]


def swap(values, axis, distance):
    count = lax.axis_size(axis)
    return lax.ppermute(values, axis, [(i, i ^ distance) for i in range(count)])


def summed_over_devices(stays, goes):
    orb_bits = [("orb", 1 << bit) for bit in range(lax.axis_size("orb").bit_length() - 1)]
    grid_bits = [("grid", 1 << bit) for bit in range(lax.axis_size("grid").bit_length() - 1)]
    half = (stays.shape[0], LANES)
    quarter = (stays.shape[0] // 2, LANES)
    other = swap(goes, "orb", 1)
    stays, goes = call(
        functools.partial(share_kernel, 2), "share", [VECTORS] * 2, [quarter] * 2, [pltpu.VMEM(half, F32)], 0.1
    )(stays, other)
    term, other = stays, swap(goes, "orb", 2)
    for axis, distance in orb_bits[2:] + grid_bits:
        term = call(add_kernel, "add", [VECTORS] * 2, [quarter], [], 0.1)(term, other)[0]
        other = swap(term, axis, distance)
    term = call(add_kernel, "add", [VECTORS] * 2, [quarter], [], 0.1)(term, other)[0]
    other = swap(term, "orb", 2)
    term = call(functools.partial(join_kernel, 2), "join", [VECTORS] * 2, [half], [], 0.1)(term, other)[0]
    return term, swap(term, "orb", 1)


def half_call(body, name, step, shapes, extra, values):
    flat, pitched = pltpu.VMEM((FLAT_ROWS, LANES), F32), pltpu.VMEM((PERIODS * (LINES + 1), LANES), F32)
    scratch = [flat, pitched, pltpu.SemaphoreType.DMA, pltpu.VMEM((YP * XP, LANES), F32)]
    scratch += [pltpu.VMEM((YP * XS, LANES), F32), pltpu.VMEM((XP * YS, LANES), F32)] + extra
    specs = [VECTORS] * 9 + [FAR] + [VECTORS] * (len(values) - 10)
    return call(functools.partial(body, step), name, specs, shapes, scratch, 3)(*values)


def first_half(step, *shared):
    return half_call(first_half_kernel, "first_half", step, [(LINE_ROWS, LANES)] * 2, [], shared)


def second_half(step, *shared):
    line = pltpu.VMEM((LINE_ROWS, LANES), F32)
    return half_call(second_half_kernel, "second_half", step, [(SENT_ROWS, LANES)], [line], shared)[0]


def per_device(ground_orbitals, occupation_signs, response_orbitals, window_offsets, ground_density):
    assert ground_orbitals.shape == (4, POINTS) and response_orbitals.shape[0] == 1
    basis_x, basis_y, basis_z = real_basis(NX), real_basis(NY), real_basis(NZ)
    tables = (
        lane_table(basis_z.T), lane_table(basis_z),
        row_table(basis_y, YP), row_table(basis_y.T, YP),
        row_table(basis_x, XP), row_table(basis_x.T, XP),
        kernel_table(),
    )
    tables = tuple(jnp.asarray(table) for table in tables)
    flat = (SENT_ROWS, LANES)
    half = (SENT_ROWS // 2, LANES)
    scratch = [pltpu.VMEM((2, 1, POINTS), F32), pltpu.SMEM((4,), jnp.int32), pltpu.SMEM((1, 2), jnp.int32)]
    stays, goes, own, kept, weights = call(
        prelude_kernel, "prelude", [FAR] * 4, [half] * 2 + [flat] * 2 + [(8, LANES)],
        scratch + [pltpu.VMEM(flat, F32), pltpu.SemaphoreType.DMA((6,))], 1,
    )(occupation_signs, window_offsets, ground_orbitals, response_orbitals)
    count = lax.axis_size("orb")
    visiting = lax.ppermute(kept, "orb", [((i + 1) % count, i) for i in range(count)])
    mine, other = summed_over_devices(stays, goes)
    low_lines, high_lines = call(
        lines_kernel, "lines", [VECTORS], [(LINE_ROWS, LANES)] * 2,
        [pltpu.VMEM((4, FLAT_ROWS, LANES), F32), pltpu.VMEM((PERIODS * (LINES + 1), LANES), F32),
         pltpu.SemaphoreType.DMA((4,))], 2,
    )(ground_orbitals)
    coefficient = call(
        coefficient_kernel, "coefficient", [FAR, VECTORS], [flat],
        [pltpu.VMEM((POINTS,), F32), pltpu.SemaphoreType.DMA], 1,
    )(ground_density, own)[0]
    values, partial = first_half(0, weights, low_lines, kept, *tables)
    away_values, away_partial = first_half(1, weights, low_lines, visiting, *tables)
    away = second_half(1, weights, high_lines, visiting, *tables, away_values, away_partial)
    second = lax.ppermute(away, "orb", [(i, (i + 1) % count) for i in range(count)])
    values, away = lax.optimization_barrier((values, away))
    first = second_half(0, weights, high_lines, kept, *tables, values, partial)
    return call(finish_kernel, "finish", [VECTORS] * 5, [(1, POINTS)], [pltpu.VMEM(flat, F32)], 1)(
        coefficient, mine, other, first, second
    )[0]


def solution(mesh):
    placed = (P("orb", None), P("orb"), P(("orb", "grid"), None), P(("orb", "grid"), None), P())
    return jax.shard_map(
        per_device, mesh=mesh, in_specs=placed, out_specs=P(("orb", "grid"), None), check_vma=False
    )
```

```python
import functools
import math

import numpy as np

import jax
import jax.numpy as jnp
from jax import lax
from jax.experimental import pallas as pl
from jax.experimental.pallas import tpu as pltpu
from jax.sharding import PartitionSpec as P


NX = 30
NY = 45
NZ = 60
SPACING = 0.5
SCREEN = 0.5
XC_COEF = 0.3282
HYBRID = 0.25

F32 = jnp.float32
BF16 = jnp.bfloat16
LANES = 128
POINTS = NX * NY * NZ
XP = 32
YP = 48
ZP = LANES // 2
XS = XP + 1
YS = YP + 1
LINES = math.lcm(NZ, LANES) // NZ
CHUNKS = math.lcm(NZ, LANES) // LANES
PERIODS = -(-NX * NY // LINES)
LINE_ROWS = PERIODS * LINES
FLAT_ROWS = PERIODS * CHUNKS
WHOLE = POINTS // LANES
TAIL = POINTS - WHOLE * LANES
SENT_ROWS = 640


def real_basis(count):
    waves = np.arange(count)
    folded = np.where(waves <= count // 2, waves, count - waves)
    angle = 2.0 * np.pi * np.outer(folded, waves) / count
    basis = np.where((waves <= count // 2)[:, None], np.cos(angle), np.sin(angle))
    return basis / np.sqrt(np.sum(basis**2, 1, keepdims=True))


def split_table(table):
    table = table.astype(np.float32)
    high = table.astype(jnp.bfloat16)
    return high, (table - high.astype(np.float32)).astype(jnp.bfloat16)


def padded(table, size):
    return np.pad(table, ((0, size - table.shape[0]), (0, size - table.shape[1])))


def lane_table(matrix):
    high, low = (np.kron(np.eye(2, dtype=jnp.bfloat16), padded(part, ZP)) for part in split_table(matrix))
    return np.block([[high, low], [high, np.zeros_like(low)]])


def row_table(matrix, size):
    high, low = (padded(part, size) for part in split_table(matrix))
    return np.concatenate([high, high, low], 1)


def kernel_table():
    def squares(count):
        places = np.arange(count)
        folded = np.where(places <= count // 2, places, places - count)
        waves = folded.astype(np.float32) * np.float32(2.0 * math.pi / (count * SPACING))
        return waves * waves

    squared = squares(NX)[None, :, None] + squares(NY)[:, None, None] + squares(NZ)[None, None, :]
    table = np.zeros((YP, XP, 2, ZP), np.float32)
    table[:NY, :NX, :, :NZ] = (4.0 * math.pi / (squared + SCREEN * SCREEN))[:, :, None, :]
    return table.reshape(YP * XP, LANES)


def split(values):
    high = values.astype(BF16)
    return high, (values - high.astype(F32)).astype(BF16)


def lane_product(values, table):
    high, low = split(values)
    halves = []
    for start in range(0, values.shape[1], LANES):
        lanes = slice(start, start + LANES)
        both = jnp.dot(jnp.concatenate([high[:, lanes], low[:, lanes]], 1), table, preferred_element_type=F32)
        halves.append(both[:, :LANES] + both[:, LANES:])
    return jnp.concatenate(halves, 1)


def row_product(table, values):
    high, low = split(values)
    return jnp.dot(table, jnp.concatenate([high, low, high], 0), preferred_element_type=F32)


def lane_ids(rows):
    return lax.broadcasted_iota(jnp.int32, (rows, LANES), 1)


def turned(values, shift):
    shift %= LANES
    return pltpu.roll(values, shift, 1) if shift else values


def line_of(flat, line, place):
    chunk, start = divmod(NZ * line, LANES)
    first = turned(flat[pl.ds(chunk, PERIODS, stride=CHUNKS), :], place - start)
    if start + NZ <= LANES:
        return first
    second = turned(flat[pl.ds(chunk + 1, PERIODS, stride=CHUNKS), :], place - start)
    return jnp.where(lane_ids(PERIODS) < place + LANES - start, first, second)


def to_lines(left, right, lines, pitched):
    ids = lane_ids(PERIODS)
    for line in range(LINES):
        low, high = line_of(left, line, 0), line_of(right, line, ZP)
        both = jnp.where(ids < NZ, low, jnp.where((ids >= ZP) & (ids < ZP + NZ), high, 0.0))
        pitched[pl.ds(line, PERIODS, stride=LINES + 1), :] = both
    for period in range(PERIODS):
        lines[pl.ds(period * LINES, LINES), :] = pitched[pl.ds(period * (LINES + 1), LINES), :]


def to_flat(lines, flat, pitched):
    ids = lane_ids(PERIODS)
    for period in range(PERIODS):
        pitched[pl.ds(period * (LINES + 1), LINES), :] = lines[pl.ds(period * LINES, LINES), :]
    for chunk in range(CHUNKS):
        low = chunk * LANES
        merged = None
        for line in range(low // NZ, -(-(low + LANES) // NZ)):
            value = turned(pitched[pl.ds(line, PERIODS, stride=LINES + 1), :], NZ * line - low)
            merged = value if merged is None else jnp.where(ids >= NZ * line - low, value, merged)
        flat[pl.ds(chunk, PERIODS, stride=CHUNKS), :] = merged


def body_copy(row, flat, sem):
    target = flat.at[pl.ds(0, WHOLE), :].reshape(1, WHOLE * LANES)
    return pltpu.make_async_copy(row.at[:, pl.ds(0, WHOLE * LANES)], target, sem)


def fill_tail(tail, flat):
    flat[pl.ds(WHOLE, flat.shape[0] - WHOLE), :] = jnp.zeros((flat.shape[0] - WHOLE, LANES), F32)
    flat[pl.ds(WHOLE, 1), pl.ds(0, TAIL)] = tail


def grouped(count, group, body):
    lax.fori_loop(0, count // group, lambda step, carry: (body(step * group), carry)[1], 0)


def prelude_kernel(signs, offsets, ground, response, stays, goes, own, kept, weights, rows, sign, offset, term, sems):
    place = lax.axis_index("grid")
    spot = pl.ds(place, 1)
    copies = [
        pltpu.make_async_copy(signs, sign, sems.at[0]),
        pltpu.make_async_copy(offsets, offset, sems.at[1]),
        body_copy(response, kept, sems.at[2]),
        pltpu.make_async_copy(response, rows.at[0], sems.at[3]),
        body_copy(ground.at[spot, :], own, sems.at[4]),
        pltpu.make_async_copy(ground.at[spot, :], rows.at[1], sems.at[5]),
    ]
    for copy in copies:
        copy.start()
    for copy in copies:
        copy.wait()
    last = pl.ds(WHOLE * LANES, TAIL)
    fill_tail(rows[0, :, last], kept)
    fill_tail(rows[1, :, last], own)
    term[...] = sign[place].astype(F32) * own[...] * kept[...]
    share(term, 1, stays, goes)
    for step in range(2):
        kept[pl.ds(SENT_ROWS - 2 + step, 1), :] = jnp.full((1, LANES), offset[0, step].astype(F32))
    ids = lane_ids(1)
    for half in range(2):
        pair = jnp.where(ids < ZP, sign[2 * half].astype(F32), sign[2 * half + 1].astype(F32))
        weights[pl.ds(half, 1), :] = pair


def lines_kernel(ground, low_lines, high_lines, flats, pitched, sems):
    copies = [body_copy(ground.at[pl.ds(j, 1), :], flats.at[j], sems.at[j]) for j in range(4)]
    for copy in copies:
        copy.start()
    for j in range(4):
        copies[j].wait()
        fill_tail(ground[pl.ds(j, 1), pl.ds(WHOLE * LANES, TAIL)], flats.at[j])
    to_lines(flats.at[0], flats.at[1], low_lines, pitched)
    to_lines(flats.at[2], flats.at[3], high_lines, pitched)


def coefficient_kernel(density, own, coefficient, values, sem):
    copy = pltpu.make_async_copy(density, values, sem)
    copy.start()
    copy.wait()
    block = 8 * LANES
    for start in range(0, POINTS, block):
        size = min(block, POINTS - start)
        shape = (8, LANES) if size == block else (1, size)
        value = values[pl.ds(start, size)].reshape(shape)
        value = -XC_COEF * jnp.exp(jnp.log(value) * (-2.0 / 3.0))
        spot = (pl.ds(start // LANES, shape[0]), pl.ds(0, shape[1]))
        coefficient[spot] = value * own[spot]


def solve_half(half, step, weights, lines, values, response, tables, kernel_copy, scratch, total, prior):
    kernel, waves, turned_waves = scratch
    z_table, z_back, y_table, y_back, x_table, x_back = (table[...] for table in tables)
    group = 15
    for x in range(NX, XP):
        waves[pl.ds(x, YP, stride=XS), :] = jnp.zeros((YP, LANES), F32)
    for y in range(NY, YP):
        turned_waves[pl.ds(y, XP, stride=YS), :] = jnp.zeros((XP, LANES), F32)

    def forward(x):
        spots = [pl.ds((x + u) * NY, YP) for u in range(group)]
        value = lane_product(jnp.concatenate([lines[spot, :] * values[spot, :] for spot in spots], 0), z_table)
        value = row_product(y_table, jnp.concatenate([value[u * YP : (u + 1) * YP] for u in range(group)], 1))
        for u in range(group):
            waves[pl.ds(x + u, YP, stride=XS), :] = value[:, u * LANES : (u + 1) * LANES]

    def middle(y):
        spots = [pl.ds(pl.multiple_of((y + u) * XP, XP), XP) for u in range(group)]
        value = row_product(x_table, jnp.concatenate([waves[pl.ds((y + u) * XS, XP), :] for u in range(group)], 1))
        value = row_product(x_back, value * jnp.concatenate([kernel[spot, :] for spot in spots], 1))
        for u in range(group):
            turned_waves[pl.ds(y + u, XP, stride=YS), :] = value[:, u * LANES : (u + 1) * LANES]

    orbital = 2 * half + (lane_ids(1) >= ZP).astype(jnp.int32)
    offset = response[pl.ds(SENT_ROWS - 2 + step, 1), :]
    factor = jnp.where(orbital.astype(F32) >= offset, weights[pl.ds(half, 1), :], 0.0)

    def backward(x):
        spots = [pl.ds((x + u) * YS, YP) for u in range(group)]
        value = row_product(y_back, jnp.concatenate([turned_waves[spot, :] for spot in spots], 1))
        value = jnp.concatenate([value[:, u * LANES : (u + 1) * LANES] for u in range(group)], 0)
        value = lane_product(value, z_back)
        for u in range(group):
            spot = pl.ds((x + u) * NY, YP)
            part = value[u * YP : (u + 1) * YP] * (lines[spot, :] * factor)
            if prior is not None:
                part += prior[spot, :]
                part += pltpu.roll(part, ZP, 1)
            total[spot, :] = part

    grouped(NX, group, forward)
    kernel_copy.wait()
    grouped(NY, group, middle)
    grouped(NX, group, backward)


def first_half_kernel(step, weights, lines, response, *refs):
    tables, (kernel, values, partial, flat, pitched, sem, *scratch) = refs[:6], refs[6:]
    kernel_copy = pltpu.make_async_copy(kernel, scratch[0], sem)
    kernel_copy.start()
    flat[pl.ds(0, WHOLE + 1), :] = response[pl.ds(0, WHOLE + 1), :]
    flat[pl.ds(WHOLE + 1, FLAT_ROWS - WHOLE - 1), :] = jnp.zeros((FLAT_ROWS - WHOLE - 1, LANES), F32)
    to_lines(flat, flat, values, pitched)
    solve_half(0, step, weights, lines, values, response, tables, kernel_copy, scratch, partial, None)


def second_half_kernel(step, weights, lines, response, *refs):
    tables, (kernel, values, partial, exchange, flat, pitched, sem, *scratch, total) = refs[:6], refs[6:]
    kernel_copy = pltpu.make_async_copy(kernel, scratch[0], sem)
    kernel_copy.start()
    solve_half(1, step, weights, lines, values, response, tables, kernel_copy, scratch, total, partial)
    to_flat(total, flat, pitched)
    exchange[...] = flat[pl.ds(0, SENT_ROWS), :]


def finish_kernel(coefficient, mine, other, first, second, out, density):
    join_kernel(1, mine, other, density)
    value = coefficient[...] * density[...] - HYBRID * (first[...] + second[...])
    out.at[:, pl.ds(0, WHOLE * LANES)].reshape(WHOLE, LANES)[...] = value[:WHOLE]
    out[:, pl.ds(WHOLE * LANES, TAIL)] = value[WHOLE : WHOLE + 1, :TAIL]


SCALARS = pl.BlockSpec(memory_space=pltpu.SMEM)
VECTORS = pl.BlockSpec(memory_space=pltpu.VMEM)
FAR = pl.BlockSpec(memory_space=pltpu.HBM)


def near(shape):
    return pltpu.VMEM(shape, F32) if shape != (1, POINTS) else jax.ShapeDtypeStruct(shape, F32)


def placed(values, spec):
    space = {id(FAR): pltpu.HBM, id(VECTORS): pltpu.VMEM}.get(id(spec))
    return values if space is None else pltpu.with_memory_space_constraint(values, space)


def call(body, specs, shapes, scratch, microseconds):
    cost = pl.CostEstimate(flops=int(microseconds * 1e9), bytes_accessed=int(microseconds * 1e6), transcendentals=0)
    kernel = pl.pallas_call(
        body,
        in_specs=specs,
        out_shape=[near(shape) for shape in shapes],
        out_specs=[VECTORS] * len(shapes),
        scratch_shapes=scratch,
        cost_estimate=cost,
        compiler_params=pltpu.CompilerParams(vmem_limit_bytes=12 * 2**20),
    )
    return lambda *values: kernel(*(placed(v, spec) for spec, v in zip(specs, values)))


def orb_bit(distance):
    return lax.rem(lax.div(lax.axis_index("orb"), distance), 2)


def share(term, distance, stays, goes):
    half, bit = stays.shape[0], orb_bit(distance)
    stays[...] = term[pl.ds(pl.multiple_of(bit * half, half), half), :]
    goes[...] = term[pl.ds(pl.multiple_of((1 - bit) * half, half), half), :]


def share_kernel(distance, mine, other, stays, goes, term):
    term[...] = mine[...] + other[...]
    share(term, distance, stays, goes)


def add_kernel(mine, other, out):
    out[...] = mine[...] + other[...]


def join_kernel(distance, mine, other, out):
    half, bit = mine.shape[0], orb_bit(distance)
    out[pl.ds(pl.multiple_of(bit * half, half), half), :] = mine[...]
    out[pl.ds(pl.multiple_of((1 - bit) * half, half), half), :] = other[...]


def swap(values, axis, distance):
    count = lax.axis_size(axis)
    return lax.ppermute(values, axis, [(i, i ^ distance) for i in range(count)])


def summed_over_devices(stays, goes):
    orb_bits = [("orb", 1 << bit) for bit in range(lax.axis_size("orb").bit_length() - 1)]
    grid_bits = [("grid", 1 << bit) for bit in range(lax.axis_size("grid").bit_length() - 1)]
    half = (stays.shape[0], LANES)
    quarter = (stays.shape[0] // 2, LANES)
    other = swap(goes, "orb", 1)
    stays, goes = call(
        functools.partial(share_kernel, 2), [VECTORS] * 2, [quarter] * 2, [pltpu.VMEM(half, F32)], 0.1
    )(stays, other)
    term, other = stays, swap(goes, "orb", 2)
    rest = orb_bits[2:] + grid_bits
    for axis, distance in rest:
        term = call(add_kernel, [VECTORS] * 2, [quarter], [], 0.1)(term, other)[0]
        other = swap(term, axis, distance)
    term = call(add_kernel, [VECTORS] * 2, [quarter], [], 0.1)(term, other)[0]
    other = swap(term, "orb", 2)
    term = call(functools.partial(join_kernel, 2), [VECTORS] * 2, [half], [], 0.1)(term, other)[0]
    return term, swap(term, "orb", 1)


def half_call(body, step, shapes, extra, values):
    flat, pitched = pltpu.VMEM((FLAT_ROWS, LANES), F32), pltpu.VMEM((PERIODS * (LINES + 1), LANES), F32)
    scratch = [flat, pitched, pltpu.SemaphoreType.DMA, pltpu.VMEM((YP * XP, LANES), F32)]
    scratch += [pltpu.VMEM((YP * XS, LANES), F32), pltpu.VMEM((XP * YS, LANES), F32)] + extra
    specs = [VECTORS] * 9 + [FAR] + [VECTORS] * (len(values) - 10)
    return call(functools.partial(body, step), specs, shapes, scratch, 3)(*values)


def first_half(step, *shared):
    return half_call(first_half_kernel, step, [(LINE_ROWS, LANES)] * 2, [], shared)


def second_half(step, *shared):
    line = pltpu.VMEM((LINE_ROWS, LANES), F32)
    return half_call(second_half_kernel, step, [(SENT_ROWS, LANES)], [line], shared)[0]


def per_device(ground_orbitals, occupation_signs, response_orbitals, window_offsets, ground_density):
    assert ground_orbitals.shape == (4, POINTS) and response_orbitals.shape[0] == 1
    basis_x, basis_y, basis_z = real_basis(NX), real_basis(NY), real_basis(NZ)
    tables = (
        lane_table(basis_z.T), lane_table(basis_z),
        row_table(basis_y, YP), row_table(basis_y.T, YP),
        row_table(basis_x, XP), row_table(basis_x.T, XP),
        kernel_table(),
    )
    tables = tuple(jnp.asarray(table) for table in tables)
    flat = (SENT_ROWS, LANES)
    half = (SENT_ROWS // 2, LANES)
    scratch = [pltpu.VMEM((2, 1, POINTS), F32), pltpu.SMEM((4,), jnp.int32), pltpu.SMEM((1, 2), jnp.int32)]
    stays, goes, own, kept, weights = call(
        prelude_kernel, [FAR] * 4, [half] * 2 + [flat] * 2 + [(8, LANES)],
        scratch + [pltpu.VMEM(flat, F32), pltpu.SemaphoreType.DMA((6,))], 1,
    )(occupation_signs, window_offsets, ground_orbitals, response_orbitals)
    count = lax.axis_size("orb")
    visiting = lax.ppermute(kept, "orb", [((i + 1) % count, i) for i in range(count)])
    mine, other = summed_over_devices(stays, goes)
    low_lines, high_lines = call(
        lines_kernel, [VECTORS], [(LINE_ROWS, LANES)] * 2,
        [pltpu.VMEM((4, FLAT_ROWS, LANES), F32), pltpu.VMEM((PERIODS * (LINES + 1), LANES), F32),
         pltpu.SemaphoreType.DMA((4,))], 2,
    )(ground_orbitals)
    coefficient = call(
        coefficient_kernel, [FAR, VECTORS], [flat],
        [pltpu.VMEM((POINTS,), F32), pltpu.SemaphoreType.DMA], 1,
    )(ground_density, own)[0]
    values, partial = first_half(0, weights, low_lines, kept, *tables)
    away_values, away_partial = first_half(1, weights, low_lines, visiting, *tables)
    away = second_half(1, weights, high_lines, visiting, *tables, away_values, away_partial)
    second = lax.ppermute(away, "orb", [(i, (i + 1) % count) for i in range(count)])
    first = second_half(0, weights, high_lines, kept, *tables, values, partial)
    return call(finish_kernel, [VECTORS] * 5, [(1, POINTS)], [pltpu.VMEM(flat, F32)], 1)(
        coefficient, mine, other, first, second
    )[0]


def solution(mesh):
    placed = (P("orb", None), P("orb"), P(("orb", "grid"), None), P(("orb", "grid"), None), P())
    return jax.shard_map(per_device, mesh=mesh, in_specs=placed, out_specs=P(("orb", "grid"), None), check_vma=False)
```

```python
import functools
import math

import numpy as np

import jax
import jax.numpy as jnp
from jax import lax
from jax.experimental import pallas as pl
from jax.experimental.pallas import tpu as pltpu
from jax.sharding import PartitionSpec as P


NX = 30
NY = 45
NZ = 60
SPACING = 0.5
SCREEN = 0.5
XC_COEF = 0.3282
HYBRID = 0.25

F32 = jnp.float32
BF16 = jnp.bfloat16
LANES = 128
POINTS = NX * NY * NZ
XP = 32
YP = 48
XS = XP + 1
YS = YP + 1
LINES = math.lcm(NZ, LANES) // NZ
CHUNKS = math.lcm(NZ, LANES) // LANES
PERIODS = -(-NX * NY // LINES)
LINE_ROWS = PERIODS * LINES
FLAT_ROWS = PERIODS * CHUNKS
WHOLE = POINTS // LANES
TAIL = POINTS - WHOLE * LANES
SENT_ROWS = 640


def real_basis(count):
    waves = np.arange(count)
    folded = np.where(waves <= count // 2, waves, count - waves)
    angle = 2.0 * np.pi * np.outer(folded, waves) / count
    basis = np.where((waves <= count // 2)[:, None], np.cos(angle), np.sin(angle))
    return basis / np.sqrt(np.sum(basis**2, 1, keepdims=True))


def split_table(table):
    table = table.astype(np.float32)
    high = table.astype(jnp.bfloat16)
    return high, (table - high.astype(np.float32)).astype(jnp.bfloat16)


def padded(table, size):
    return np.pad(table, ((0, size - table.shape[0]), (0, size - table.shape[1])))


def lane_table(matrix):
    high, low = (padded(np.kron(np.eye(2, dtype=jnp.bfloat16), part), LANES) for part in split_table(matrix))
    return np.block([[high, low], [high, np.zeros_like(low)]])


def row_table(matrix, size):
    high, low = (padded(part, size) for part in split_table(matrix))
    return np.concatenate([high, high, low], 1)


def kernel_table():
    def squares(count):
        places = np.arange(count)
        folded = np.where(places <= count // 2, places, places - count)
        waves = folded.astype(np.float32) * np.float32(2.0 * math.pi / (count * SPACING))
        return waves * waves

    squared = squares(NX)[None, :, None] + squares(NY)[:, None, None] + squares(NZ)[None, None, :]
    table = np.zeros((YP, XP, LANES), np.float32)
    table[:NY, :NX, : 2 * NZ] = np.tile(4.0 * math.pi / (squared + SCREEN * SCREEN), (1, 1, 2))
    return table.reshape(YP * XP, LANES)


def split(values):
    high = values.astype(BF16)
    return high, (values - high.astype(F32)).astype(BF16)


def lane_product(values, table):
    high, low = split(values)
    halves = []
    for start in range(0, values.shape[1], LANES):
        lanes = slice(start, start + LANES)
        both = jnp.dot(jnp.concatenate([high[:, lanes], low[:, lanes]], 1), table, preferred_element_type=F32)
        halves.append(both[:, :LANES] + both[:, LANES:])
    return jnp.concatenate(halves, 1)


def row_product(table, values):
    high, low = split(values)
    return jnp.dot(table, jnp.concatenate([high, low, high], 0), preferred_element_type=F32)


def lane_ids(rows):
    return lax.broadcasted_iota(jnp.int32, (rows, LANES), 1)


def turned(values, shift):
    shift %= LANES
    return pltpu.roll(values, shift, 1) if shift else values


def two_lines(flat, line, places):
    chunk, start = divmod(NZ * line, LANES)
    value = flat[pl.ds(chunk, PERIODS, stride=CHUNKS), :]
    if start + 2 * NZ > LANES:
        after = flat[pl.ds(chunk + 1, PERIODS, stride=CHUNKS), :]
        value = jnp.where(lane_ids(PERIODS) >= start, value, after)
    return [turned(value, place - start) for place in places]


def to_lines(left, right, lines, pitched):
    ids = lane_ids(PERIODS)
    for line in range(0, LINES, 2):
        if left is right:
            middle, late, early = two_lines(left, line, (0, NZ, -NZ))
            pairs = (jnp.where(ids < NZ, middle, late), jnp.where(ids < NZ, early, middle))
        else:
            (low, next_low), (high, next_high) = two_lines(left, line, (0, -NZ)), two_lines(right, line, (NZ, 0))
            pairs = (jnp.where(ids < NZ, low, high), jnp.where(ids < NZ, next_low, next_high))
        for place, pair in enumerate(pairs):
            pair = jnp.where(ids < 2 * NZ, pair, 0.0)
            pitched[pl.ds(line + place, PERIODS, stride=LINES + 1), :] = pair
    for period in range(PERIODS):
        lines[pl.ds(period * LINES, LINES), :] = pitched[pl.ds(period * (LINES + 1), LINES), :]


def to_flat(lines, flat, pitched):
    ids = lane_ids(PERIODS)
    for period in range(PERIODS):
        pitched[pl.ds(period * (LINES + 1), LINES), :] = lines[pl.ds(period * LINES, LINES), :]
    for chunk in range(CHUNKS):
        low = chunk * LANES
        merged = None
        for line in range(low // NZ, -(-(low + LANES) // NZ)):
            value = turned(pitched[pl.ds(line, PERIODS, stride=LINES + 1), :], NZ * line - low)
            merged = value if merged is None else jnp.where(ids >= NZ * line - low, value, merged)
        flat[pl.ds(chunk, PERIODS, stride=CHUNKS), :] = merged


def body_copy(row, flat, sem):
    target = flat.at[pl.ds(0, WHOLE), :].reshape(1, WHOLE * LANES)
    return pltpu.make_async_copy(row.at[:, pl.ds(0, WHOLE * LANES)], target, sem)


def fill_tail(tail, flat):
    flat[pl.ds(WHOLE, flat.shape[0] - WHOLE), :] = jnp.zeros((flat.shape[0] - WHOLE, LANES), F32)
    flat[pl.ds(WHOLE, 1), pl.ds(0, TAIL)] = tail


def grouped(count, group, body):
    lax.fori_loop(0, count // group, lambda step, carry: (body(step * group), carry)[1], 0)


def prelude_kernel(signs, offsets, ground, response, stays, goes, own, kept, weights, rows, sign, offset, term, sems):
    place = lax.axis_index("grid")
    spot = pl.ds(place, 1)
    copies = [
        pltpu.make_async_copy(signs, sign, sems.at[0]),
        pltpu.make_async_copy(offsets, offset, sems.at[1]),
        body_copy(response, kept, sems.at[2]),
        pltpu.make_async_copy(response, rows.at[0], sems.at[3]),
        body_copy(ground.at[spot, :], own, sems.at[4]),
        pltpu.make_async_copy(ground.at[spot, :], rows.at[1], sems.at[5]),
    ]
    for copy in copies:
        copy.start()
    for copy in copies:
        copy.wait()
    last = pl.ds(WHOLE * LANES, TAIL)
    fill_tail(rows[0, :, last], kept)
    fill_tail(rows[1, :, last], own)
    term[...] = sign[place].astype(F32) * own[...] * kept[...]
    share(term, 1, stays, goes)
    for step in range(2):
        kept[pl.ds(SENT_ROWS - 2 + step, 1), :] = jnp.full((1, LANES), offset[0, step].astype(F32))
    ids = lane_ids(1)
    for half in range(2):
        pair = jnp.where(ids < NZ, sign[2 * half].astype(F32), sign[2 * half + 1].astype(F32))
        weights[pl.ds(half, 1), :] = pair


def lines_kernel(ground, low_lines, high_lines, flats, pitched, sems):
    copies = [body_copy(ground.at[pl.ds(j, 1), :], flats.at[j], sems.at[j]) for j in range(4)]
    for copy in copies:
        copy.start()
    for j in range(4):
        copies[j].wait()
        fill_tail(ground[pl.ds(j, 1), pl.ds(WHOLE * LANES, TAIL)], flats.at[j])
    to_lines(flats.at[0], flats.at[1], low_lines, pitched)
    to_lines(flats.at[2], flats.at[3], high_lines, pitched)


def coefficient_kernel(density, own, coefficient, values, sem):
    copy = pltpu.make_async_copy(density, values, sem)
    copy.start()
    copy.wait()
    block = 8 * LANES
    for start in range(0, POINTS, block):
        size = min(block, POINTS - start)
        shape = (8, LANES) if size == block else (1, size)
        value = values[pl.ds(start, size)].reshape(shape)
        value = -XC_COEF * jnp.exp(jnp.log(value) * (-2.0 / 3.0))
        spot = (pl.ds(start // LANES, shape[0]), pl.ds(0, shape[1]))
        coefficient[spot] = value * own[spot]


def solve_half(half, step, weights, lines, values, response, tables, kernel_copy, scratch, total, prior):
    kernel, waves, turned_waves = scratch
    z_table, z_back, y_table, y_back, x_table, x_back = (table[...] for table in tables)
    for x in range(NX, XP):
        waves[pl.ds(x, YP, stride=XS), :] = jnp.zeros((YP, LANES), F32)
    for y in range(NY, YP):
        turned_waves[pl.ds(y, XP, stride=YS), :] = jnp.zeros((XP, LANES), F32)

    def forward(x):
        group = 15
        spots = [pl.ds((x + u) * NY, YP) for u in range(group)]
        value = lane_product(jnp.concatenate([lines[spot, :] * values[spot, :] for spot in spots], 0), z_table)
        value = row_product(y_table, jnp.concatenate([value[u * YP : (u + 1) * YP] for u in range(group)], 1))
        for u in range(group):
            waves[pl.ds(x + u, YP, stride=XS), :] = value[:, u * LANES : (u + 1) * LANES]

    def middle(y):
        group = 45
        spots = [pl.ds(pl.multiple_of((y + u) * XP, XP), XP) for u in range(group)]
        value = row_product(x_table, jnp.concatenate([waves[pl.ds((y + u) * XS, XP), :] for u in range(group)], 1))
        value = row_product(x_back, value * jnp.concatenate([kernel[spot, :] for spot in spots], 1))
        for u in range(group):
            turned_waves[pl.ds(y + u, XP, stride=YS), :] = value[:, u * LANES : (u + 1) * LANES]

    orbital = 2 * half + (lane_ids(1) >= NZ).astype(jnp.int32)
    offset = response[pl.ds(SENT_ROWS - 2 + step, 1), :]
    factor = jnp.where(orbital.astype(F32) >= offset, weights[pl.ds(half, 1), :], 0.0)

    def backward(x):
        group = 30
        spots = [pl.ds((x + u) * YS, YP) for u in range(group)]
        value = row_product(y_back, jnp.concatenate([turned_waves[spot, :] for spot in spots], 1))
        value = jnp.concatenate([value[:, u * LANES : (u + 1) * LANES] for u in range(group)], 0)
        value = lane_product(value, z_back)
        for u in range(group):
            spot = pl.ds((x + u) * NY, YP)
            part = value[u * YP : (u + 1) * YP] * (lines[spot, :] * factor)
            if prior is not None:
                part += prior[spot, :]
                part += pltpu.roll(part, LANES - NZ, 1)
            total[spot, :] = part

    grouped(NX, 15, forward)
    kernel_copy.wait()
    grouped(NY, 45, middle)
    grouped(NX, 30, backward)


def first_half_kernel(step, weights, lines, response, *refs):
    tables, (kernel, values, partial, flat, pitched, sem, *scratch) = refs[:6], refs[6:]
    kernel_copy = pltpu.make_async_copy(kernel, scratch[0], sem)
    kernel_copy.start()
    flat[pl.ds(0, WHOLE + 1), :] = response[pl.ds(0, WHOLE + 1), :]
    flat[pl.ds(WHOLE + 1, FLAT_ROWS - WHOLE - 1), :] = jnp.zeros((FLAT_ROWS - WHOLE - 1, LANES), F32)
    to_lines(flat, flat, values, pitched)
    solve_half(0, step, weights, lines, values, response, tables, kernel_copy, scratch, partial, None)


def second_half_kernel(step, weights, lines, response, *refs):
    tables, (kernel, values, partial, exchange, flat, pitched, sem, *scratch, total) = refs[:6], refs[6:]
    kernel_copy = pltpu.make_async_copy(kernel, scratch[0], sem)
    kernel_copy.start()
    solve_half(1, step, weights, lines, values, response, tables, kernel_copy, scratch, total, partial)
    to_flat(total, flat, pitched)
    exchange[...] = flat[pl.ds(0, SENT_ROWS), :]


def finish_kernel(coefficient, mine, other, first, second, out, density):
    join_kernel(1, mine, other, density)
    value = coefficient[...] * density[...] - HYBRID * (first[...] + second[...])
    out.at[:, pl.ds(0, WHOLE * LANES)].reshape(WHOLE, LANES)[...] = value[:WHOLE]
    out[:, pl.ds(WHOLE * LANES, TAIL)] = value[WHOLE : WHOLE + 1, :TAIL]


SCALARS = pl.BlockSpec(memory_space=pltpu.SMEM)
VECTORS = pl.BlockSpec(memory_space=pltpu.VMEM)
FAR = pl.BlockSpec(memory_space=pltpu.HBM)


def near(shape):
    return pltpu.VMEM(shape, F32) if shape != (1, POINTS) else jax.ShapeDtypeStruct(shape, F32)


def placed(values, spec):
    space = {id(FAR): pltpu.HBM, id(VECTORS): pltpu.VMEM}.get(id(spec))
    return values if space is None else pltpu.with_memory_space_constraint(values, space)


def call(body, specs, shapes, scratch, microseconds):
    cost = pl.CostEstimate(flops=int(microseconds * 1e9), bytes_accessed=int(microseconds * 1e6), transcendentals=0)
    kernel = pl.pallas_call(
        body,
        in_specs=specs,
        out_shape=[near(shape) for shape in shapes],
        out_specs=[VECTORS] * len(shapes),
        scratch_shapes=scratch,
        cost_estimate=cost,
        compiler_params=pltpu.CompilerParams(vmem_limit_bytes=12 * 2**20),
    )
    return lambda *values: kernel(*(placed(v, spec) for spec, v in zip(specs, values)))


def orb_bit(distance):
    return lax.rem(lax.div(lax.axis_index("orb"), distance), 2)


def share(term, distance, stays, goes):
    half, bit = stays.shape[0], orb_bit(distance)
    stays[...] = term[pl.ds(pl.multiple_of(bit * half, half), half), :]
    goes[...] = term[pl.ds(pl.multiple_of((1 - bit) * half, half), half), :]


def share_kernel(distance, mine, other, stays, goes, term):
    term[...] = mine[...] + other[...]
    share(term, distance, stays, goes)


def add_kernel(mine, other, out):
    out[...] = mine[...] + other[...]


def join_kernel(distance, mine, other, out):
    half, bit = mine.shape[0], orb_bit(distance)
    out[pl.ds(pl.multiple_of(bit * half, half), half), :] = mine[...]
    out[pl.ds(pl.multiple_of((1 - bit) * half, half), half), :] = other[...]


def swap(values, axis, distance):
    count = lax.axis_size(axis)
    return lax.ppermute(values, axis, [(i, i ^ distance) for i in range(count)])


def summed_over_devices(stays, goes):
    orb_bits = [("orb", 1 << bit) for bit in range(lax.axis_size("orb").bit_length() - 1)]
    grid_bits = [("grid", 1 << bit) for bit in range(lax.axis_size("grid").bit_length() - 1)]
    half = (stays.shape[0], LANES)
    quarter = (stays.shape[0] // 2, LANES)
    other = swap(goes, "orb", 1)
    stays, goes = call(
        functools.partial(share_kernel, 2), [VECTORS] * 2, [quarter] * 2, [pltpu.VMEM(half, F32)], 0.1
    )(stays, other)
    term, other = stays, swap(goes, "orb", 2)
    rest = orb_bits[2:] + grid_bits
    for axis, distance in rest:
        term = call(add_kernel, [VECTORS] * 2, [quarter], [], 0.1)(term, other)[0]
        other = swap(term, axis, distance)
    term = call(add_kernel, [VECTORS] * 2, [quarter], [], 0.1)(term, other)[0]
    other = swap(term, "orb", 2)
    term = call(functools.partial(join_kernel, 2), [VECTORS] * 2, [half], [], 0.1)(term, other)[0]
    return term, swap(term, "orb", 1)


def half_call(body, step, shapes, extra, values):
    flat, pitched = pltpu.VMEM((FLAT_ROWS, LANES), F32), pltpu.VMEM((PERIODS * (LINES + 1), LANES), F32)
    scratch = [flat, pitched, pltpu.SemaphoreType.DMA, pltpu.VMEM((YP * XP, LANES), F32)]
    scratch += [pltpu.VMEM((YP * XS, LANES), F32), pltpu.VMEM((XP * YS, LANES), F32)] + extra
    specs = [VECTORS] * 9 + [FAR] + [VECTORS] * (len(values) - 10)
    return call(functools.partial(body, step), specs, shapes, scratch, 3)(*values)


def first_half(step, *shared):
    return half_call(first_half_kernel, step, [(LINE_ROWS, LANES)] * 2, [], shared)


def second_half(step, *shared):
    line = pltpu.VMEM((LINE_ROWS, LANES), F32)
    return half_call(second_half_kernel, step, [(SENT_ROWS, LANES)], [line], shared)[0]


def lines_call(ground):
    return call(
        lines_kernel, [VECTORS], [(LINE_ROWS, LANES)] * 2,
        [pltpu.VMEM((4, FLAT_ROWS, LANES), F32), pltpu.VMEM((PERIODS * (LINES + 1), LANES), F32),
         pltpu.SemaphoreType.DMA((4,))], 2,
    )(ground)


def per_device(ground_orbitals, occupation_signs, response_orbitals, window_offsets, ground_density):
    assert ground_orbitals.shape == (4, POINTS) and response_orbitals.shape[0] == 1
    basis_x, basis_y, basis_z = real_basis(NX), real_basis(NY), real_basis(NZ)
    tables = (
        lane_table(basis_z.T), lane_table(basis_z),
        row_table(basis_y, YP), row_table(basis_y.T, YP),
        row_table(basis_x, XP), row_table(basis_x.T, XP),
        kernel_table(),
    )
    tables = tuple(jnp.asarray(table) for table in tables)
    flat = (SENT_ROWS, LANES)
    half = (SENT_ROWS // 2, LANES)
    scratch = [pltpu.VMEM((2, 1, POINTS), F32), pltpu.SMEM((4,), jnp.int32), pltpu.SMEM((1, 2), jnp.int32)]
    stays, goes, own, kept, weights = call(
        prelude_kernel, [FAR] * 4, [half] * 2 + [flat] * 2 + [(8, LANES)],
        scratch + [pltpu.VMEM(flat, F32), pltpu.SemaphoreType.DMA((6,))], 1,
    )(occupation_signs, window_offsets, ground_orbitals, response_orbitals)
    count = lax.axis_size("orb")
    visiting = lax.ppermute(kept, "orb", [((i + 1) % count, i) for i in range(count)])
    mine, other = summed_over_devices(stays, goes)
    low_lines, high_lines = lines_call(ground_orbitals)
    coefficient = call(
        coefficient_kernel, [FAR, VECTORS], [flat],
        [pltpu.VMEM((POINTS,), F32), pltpu.SemaphoreType.DMA], 1,
    )(ground_density, own)[0]
    values, partial = first_half(0, weights, low_lines, kept, *tables)
    away_values, away_partial = first_half(1, weights, low_lines, visiting, *tables)
    away = second_half(1, weights, high_lines, visiting, *tables, away_values, away_partial)
    second = lax.ppermute(away, "orb", [(i, (i + 1) % count) for i in range(count)])
    first = second_half(0, weights, high_lines, kept, *tables, values, partial)
    return call(finish_kernel, [VECTORS] * 5, [(1, POINTS)], [pltpu.VMEM(flat, F32)], 1)(
        coefficient, mine, other, first, second
    )[0]


def solution(mesh):
    placed = (P("orb", None), P("orb"), P(("orb", "grid"), None), P(("orb", "grid"), None), P())
    return jax.shard_map(per_device, mesh=mesh, in_specs=placed, out_specs=P(("orb", "grid"), None), check_vma=False)
```

```python
import functools
import math

import numpy as np

import jax
import jax.numpy as jnp
from jax import lax
from jax.experimental import pallas as pl
from jax.experimental.pallas import tpu as pltpu
from jax.sharding import PartitionSpec as P


NX = 30
NY = 45
NZ = 60
SPACING = 0.5
SCREEN = 0.5
XC_COEF = 0.3282
HYBRID = 0.25

F32 = jnp.float32
BF16 = jnp.bfloat16
LANES = 128
POINTS = NX * NY * NZ
XP = 32
YP = 48
XS = XP + 1
YS = YP + 1
LINES = math.lcm(NZ, LANES) // NZ
CHUNKS = math.lcm(NZ, LANES) // LANES
PERIODS = -(-NX * NY // LINES)
LINE_ROWS = PERIODS * LINES
FLAT_ROWS = PERIODS * CHUNKS
WHOLE = POINTS // LANES
TAIL = POINTS - WHOLE * LANES
SENT_ROWS = 640


def real_basis(count):
    waves = np.arange(count)
    folded = np.where(waves <= count // 2, waves, count - waves)
    angle = 2.0 * np.pi * np.outer(folded, waves) / count
    basis = np.where((waves <= count // 2)[:, None], np.cos(angle), np.sin(angle))
    return basis / np.sqrt(np.sum(basis**2, 1, keepdims=True))


def split_table(table):
    table = table.astype(np.float32)
    high = table.astype(jnp.bfloat16)
    return high, (table - high.astype(np.float32)).astype(jnp.bfloat16)


def padded(table, size):
    return np.pad(table, ((0, size - table.shape[0]), (0, size - table.shape[1])))


def lane_table(matrix):
    high, low = (padded(np.kron(np.eye(2, dtype=jnp.bfloat16), part), LANES) for part in split_table(matrix))
    return np.block([[high, low], [high, np.zeros_like(low)]])


def row_table(matrix, size):
    high, low = (padded(part, size) for part in split_table(matrix))
    return np.concatenate([high, high, low], 1)


def kernel_table():
    def squares(count):
        places = np.arange(count)
        folded = np.where(places <= count // 2, places, places - count)
        waves = folded.astype(np.float32) * np.float32(2.0 * math.pi / (count * SPACING))
        return waves * waves

    squared = squares(NX)[None, :, None] + squares(NY)[:, None, None] + squares(NZ)[None, None, :]
    table = np.zeros((YP, XP, LANES), np.float32)
    table[:NY, :NX, : 2 * NZ] = np.tile(4.0 * math.pi / (squared + SCREEN * SCREEN), (1, 1, 2))
    return table.reshape(YP * XP, LANES)


def split(values):
    high = values.astype(BF16)
    return high, (values - high.astype(F32)).astype(BF16)


def lane_product(values, table):
    high, low = split(values)
    halves = []
    for start in range(0, values.shape[1], LANES):
        lanes = slice(start, start + LANES)
        both = jnp.dot(jnp.concatenate([high[:, lanes], low[:, lanes]], 1), table, preferred_element_type=F32)
        halves.append(both[:, :LANES] + both[:, LANES:])
    return jnp.concatenate(halves, 1)


def row_product(table, values):
    high, low = split(values)
    return jnp.dot(table, jnp.concatenate([high, low, high], 0), preferred_element_type=F32)


def lane_ids(rows):
    return lax.broadcasted_iota(jnp.int32, (rows, LANES), 1)


def turned(values, shift):
    shift %= LANES
    return pltpu.roll(values, shift, 1) if shift else values


def two_lines(flat, line, places):
    chunk, start = divmod(NZ * line, LANES)
    value = flat[pl.ds(chunk, PERIODS, stride=CHUNKS), :]
    if start + 2 * NZ > LANES:
        after = flat[pl.ds(chunk + 1, PERIODS, stride=CHUNKS), :]
        value = jnp.where(lane_ids(PERIODS) >= start, value, after)
    return [turned(value, place - start) for place in places]


def to_lines(left, right, lines, pitched):
    ids = lane_ids(PERIODS)
    for line in range(0, LINES, 2):
        if left is right:
            middle, late, early = two_lines(left, line, (0, NZ, -NZ))
            pairs = (jnp.where(ids < NZ, middle, late), jnp.where(ids < NZ, early, middle))
        else:
            (low, next_low), (high, next_high) = two_lines(left, line, (0, -NZ)), two_lines(right, line, (NZ, 0))
            pairs = (jnp.where(ids < NZ, low, high), jnp.where(ids < NZ, next_low, next_high))
        for place, pair in enumerate(pairs):
            pair = jnp.where(ids < 2 * NZ, pair, 0.0)
            pitched[pl.ds(line + place, PERIODS, stride=LINES + 1), :] = pair
    for period in range(PERIODS):
        lines[pl.ds(period * LINES, LINES), :] = pitched[pl.ds(period * (LINES + 1), LINES), :]


def to_flat(lines, flat, pitched):
    ids = lane_ids(PERIODS)
    for period in range(PERIODS):
        pitched[pl.ds(period * (LINES + 1), LINES), :] = lines[pl.ds(period * LINES, LINES), :]
    for chunk in range(CHUNKS):
        low = chunk * LANES
        merged = None
        for line in range(low // NZ, -(-(low + LANES) // NZ)):
            value = turned(pitched[pl.ds(line, PERIODS, stride=LINES + 1), :], NZ * line - low)
            merged = value if merged is None else jnp.where(ids >= NZ * line - low, value, merged)
        flat[pl.ds(chunk, PERIODS, stride=CHUNKS), :] = merged


def body_copy(row, flat, sem):
    target = flat.at[pl.ds(0, WHOLE), :].reshape(1, WHOLE * LANES)
    return pltpu.make_async_copy(row.at[:, pl.ds(0, WHOLE * LANES)], target, sem)


def fill_tail(tail, flat):
    flat[pl.ds(WHOLE, flat.shape[0] - WHOLE), :] = jnp.zeros((flat.shape[0] - WHOLE, LANES), F32)
    flat[pl.ds(WHOLE, 1), pl.ds(0, TAIL)] = tail


def grouped(count, group, body):
    lax.fori_loop(0, count // group, lambda step, carry: (body(step * group), carry)[1], 0)


def prelude_kernel(signs, offsets, ground, response, stays, goes, own, kept, weights, rows, sign, offset, term, sems):
    place = lax.axis_index("grid")
    spot = pl.ds(place, 1)
    copies = [
        pltpu.make_async_copy(signs, sign, sems.at[0]),
        pltpu.make_async_copy(offsets, offset, sems.at[1]),
        body_copy(response, kept, sems.at[2]),
        pltpu.make_async_copy(response, rows.at[0], sems.at[3]),
        body_copy(ground.at[spot, :], own, sems.at[4]),
        pltpu.make_async_copy(ground.at[spot, :], rows.at[1], sems.at[5]),
    ]
    for copy in copies:
        copy.start()
    for copy in copies:
        copy.wait()
    last = pl.ds(WHOLE * LANES, TAIL)
    fill_tail(rows[0, :, last], kept)
    fill_tail(rows[1, :, last], own)
    term[...] = sign[place].astype(F32) * own[...] * kept[...]
    share(term, 1, stays, goes)
    for step in range(2):
        kept[pl.ds(SENT_ROWS - 2 + step, 1), :] = jnp.full((1, LANES), offset[0, step].astype(F32))
    ids = lane_ids(1)
    for half in range(2):
        pair = jnp.where(ids < NZ, sign[2 * half].astype(F32), sign[2 * half + 1].astype(F32))
        weights[pl.ds(half, 1), :] = pair


def lines_kernel(ground, low_lines, high_lines, flats, pitched, sems):
    copies = [body_copy(ground.at[pl.ds(j, 1), :], flats.at[j], sems.at[j]) for j in range(4)]
    for copy in copies:
        copy.start()
    for j in range(4):
        copies[j].wait()
        fill_tail(ground[pl.ds(j, 1), pl.ds(WHOLE * LANES, TAIL)], flats.at[j])
    to_lines(flats.at[0], flats.at[1], low_lines, pitched)
    to_lines(flats.at[2], flats.at[3], high_lines, pitched)


def coefficient_kernel(density, own, coefficient, values, sem):
    copy = pltpu.make_async_copy(density, values, sem)
    copy.start()
    copy.wait()
    block = 8 * LANES
    for start in range(0, POINTS, block):
        size = min(block, POINTS - start)
        shape = (8, LANES) if size == block else (1, size)
        value = values[pl.ds(start, size)].reshape(shape)
        value = -XC_COEF * jnp.exp(jnp.log(value) * (-2.0 / 3.0))
        spot = (pl.ds(start // LANES, shape[0]), pl.ds(0, shape[1]))
        coefficient[spot] = value * own[spot]


def solve_half(half, step, weights, lines, values, response, tables, kernel_copy, scratch, total, prior):
    kernel, waves, turned_waves = scratch
    z_table, z_back, y_table, y_back, x_table, x_back = (table[...] for table in tables)
    for x in range(NX, XP):
        waves[pl.ds(x, YP, stride=XS), :] = jnp.zeros((YP, LANES), F32)
    for y in range(NY, YP):
        turned_waves[pl.ds(y, XP, stride=YS), :] = jnp.zeros((XP, LANES), F32)

    def forward(x):
        group = 15
        spots = [pl.ds((x + u) * NY, YP) for u in range(group)]
        value = lane_product(jnp.concatenate([lines[spot, :] * values[spot, :] for spot in spots], 0), z_table)
        value = row_product(y_table, jnp.concatenate([value[u * YP : (u + 1) * YP] for u in range(group)], 1))
        for u in range(group):
            waves[pl.ds(x + u, YP, stride=XS), :] = value[:, u * LANES : (u + 1) * LANES]

    def middle(y):
        group = 45
        spots = [pl.ds(pl.multiple_of((y + u) * XP, XP), XP) for u in range(group)]
        value = row_product(x_table, jnp.concatenate([waves[pl.ds((y + u) * XS, XP), :] for u in range(group)], 1))
        value = row_product(x_back, value * jnp.concatenate([kernel[spot, :] for spot in spots], 1))
        for u in range(group):
            turned_waves[pl.ds(y + u, XP, stride=YS), :] = value[:, u * LANES : (u + 1) * LANES]

    orbital = 2 * half + (lane_ids(1) >= NZ).astype(jnp.int32)
    offset = response[pl.ds(SENT_ROWS - 2 + step, 1), :]
    factor = jnp.where(orbital.astype(F32) >= offset, weights[pl.ds(half, 1), :], 0.0)

    def backward(x):
        group = 30
        spots = [pl.ds((x + u) * YS, YP) for u in range(group)]
        value = row_product(y_back, jnp.concatenate([turned_waves[spot, :] for spot in spots], 1))
        value = jnp.concatenate([value[:, u * LANES : (u + 1) * LANES] for u in range(group)], 0)
        value = lane_product(value, z_back)
        for u in range(group):
            spot = pl.ds((x + u) * NY, YP)
            part = value[u * YP : (u + 1) * YP] * (lines[spot, :] * factor)
            if prior is not None:
                part += prior[spot, :]
                part += pltpu.roll(part, LANES - NZ, 1)
            total[spot, :] = part

    grouped(NX, 15, forward)
    kernel_copy.wait()
    grouped(NY, 45, middle)
    grouped(NX, 30, backward)


def first_half_kernel(step, weights, lines, response, *refs):
    tables, (kernel, values, partial, flat, pitched, sem, *scratch) = refs[:6], refs[6:]
    kernel_copy = pltpu.make_async_copy(kernel, scratch[0], sem)
    kernel_copy.start()
    flat[pl.ds(0, WHOLE + 1), :] = response[pl.ds(0, WHOLE + 1), :]
    flat[pl.ds(WHOLE + 1, FLAT_ROWS - WHOLE - 1), :] = jnp.zeros((FLAT_ROWS - WHOLE - 1, LANES), F32)
    to_lines(flat, flat, values, pitched)
    solve_half(0, step, weights, lines, values, response, tables, kernel_copy, scratch, partial, None)


def second_half_kernel(step, weights, lines, response, *refs):
    tables, (kernel, values, partial, exchange, flat, pitched, sem, *scratch, total) = refs[:6], refs[6:]
    kernel_copy = pltpu.make_async_copy(kernel, scratch[0], sem)
    kernel_copy.start()
    solve_half(1, step, weights, lines, values, response, tables, kernel_copy, scratch, total, partial)
    to_flat(total, flat, pitched)
    exchange[...] = flat[pl.ds(0, SENT_ROWS), :]


def finish_kernel(coefficient, mine, other, first, second, out, density):
    join_kernel(1, mine, other, density)
    value = coefficient[...] * density[...] - HYBRID * (first[...] + second[...])
    out.at[:, pl.ds(0, WHOLE * LANES)].reshape(WHOLE, LANES)[...] = value[:WHOLE]
    out[:, pl.ds(WHOLE * LANES, TAIL)] = value[WHOLE : WHOLE + 1, :TAIL]


SCALARS = pl.BlockSpec(memory_space=pltpu.SMEM)
VECTORS = pl.BlockSpec(memory_space=pltpu.VMEM)
FAR = pl.BlockSpec(memory_space=pltpu.HBM)


def near(shape):
    return pltpu.VMEM(shape, F32) if shape != (1, POINTS) else jax.ShapeDtypeStruct(shape, F32)


def placed(values, spec):
    space = {id(FAR): pltpu.HBM, id(VECTORS): pltpu.VMEM}.get(id(spec))
    return values if space is None else pltpu.with_memory_space_constraint(values, space)


def call(body, specs, shapes, scratch, microseconds):
    cost = pl.CostEstimate(flops=int(microseconds * 1e9), bytes_accessed=int(microseconds * 1e6), transcendentals=0)
    kernel = pl.pallas_call(
        body,
        in_specs=specs,
        out_shape=[near(shape) for shape in shapes],
        out_specs=[VECTORS] * len(shapes),
        scratch_shapes=scratch,
        cost_estimate=cost,
        compiler_params=pltpu.CompilerParams(vmem_limit_bytes=12 * 2**20),
    )
    return lambda *values: kernel(*(placed(v, spec) for spec, v in zip(specs, values)))


def orb_bit(distance):
    return lax.rem(lax.div(lax.axis_index("orb"), distance), 2)


def share(term, distance, stays, goes):
    half, bit = stays.shape[0], orb_bit(distance)
    stays[...] = term[pl.ds(pl.multiple_of(bit * half, half), half), :]
    goes[...] = term[pl.ds(pl.multiple_of((1 - bit) * half, half), half), :]


def add_kernel(mine, other, out):
    out[...] = mine[...] + other[...]


def join_kernel(distance, mine, other, out):
    half, bit = mine.shape[0], orb_bit(distance)
    out[pl.ds(pl.multiple_of(bit * half, half), half), :] = mine[...]
    out[pl.ds(pl.multiple_of((1 - bit) * half, half), half), :] = other[...]


def swap(values, partner):
    orbs, grids = lax.axis_size("orb"), lax.axis_size("grid")
    pairs = []
    for orb in range(orbs):
        for grid in range(grids):
            axis, distance = partner(orb)
            to = (orb ^ distance, grid) if axis == "orb" else (orb, grid ^ distance)
            pairs.append((orb * grids + grid, to[0] * grids + to[1]))
    return lax.ppermute(values, ("orb", "grid"), pairs)


def added(mine, other):
    return call(add_kernel, [VECTORS] * 2, [mine.shape], [], 0.1)(mine, other)[0]


def summed_over_devices(stays, goes):
    steps = [("orb", 1 << bit) for bit in range(1, lax.axis_size("orb").bit_length() - 1)]
    steps += [("grid", 1 << bit) for bit in range(lax.axis_size("grid").bit_length() - 1)]
    turn = len(steps) // 2
    orders = (steps, steps[turn:] + steps[:turn])
    other = swap(goes, lambda orb: ("orb", 1))
    term = added(stays, other)
    for place in range(len(steps)):
        other = swap(term, lambda orb: orders[orb % 2][place])
        term = added(term, other)
    return term, swap(term, lambda orb: ("orb", 1))


def half_call(body, step, shapes, extra, values):
    flat, pitched = pltpu.VMEM((FLAT_ROWS, LANES), F32), pltpu.VMEM((PERIODS * (LINES + 1), LANES), F32)
    scratch = [flat, pitched, pltpu.SemaphoreType.DMA, pltpu.VMEM((YP * XP, LANES), F32)]
    scratch += [pltpu.VMEM((YP * XS, LANES), F32), pltpu.VMEM((XP * YS, LANES), F32)] + extra
    specs = [VECTORS] * 9 + [FAR] + [VECTORS] * (len(values) - 10)
    return call(functools.partial(body, step), specs, shapes, scratch, 3)(*values)


def first_half(step, *shared):
    return half_call(first_half_kernel, step, [(LINE_ROWS, LANES)] * 2, [], shared)


def second_half(step, *shared):
    line = pltpu.VMEM((LINE_ROWS, LANES), F32)
    return half_call(second_half_kernel, step, [(SENT_ROWS, LANES)], [line], shared)[0]


def lines_call(ground):
    return call(
        lines_kernel, [VECTORS], [(LINE_ROWS, LANES)] * 2,
        [pltpu.VMEM((4, FLAT_ROWS, LANES), F32), pltpu.VMEM((PERIODS * (LINES + 1), LANES), F32),
         pltpu.SemaphoreType.DMA((4,))], 2,
    )(ground)


def per_device(ground_orbitals, occupation_signs, response_orbitals, window_offsets, ground_density):
    assert ground_orbitals.shape == (4, POINTS) and response_orbitals.shape[0] == 1
    basis_x, basis_y, basis_z = real_basis(NX), real_basis(NY), real_basis(NZ)
    tables = (
        lane_table(basis_z.T), lane_table(basis_z),
        row_table(basis_y, YP), row_table(basis_y.T, YP),
        row_table(basis_x, XP), row_table(basis_x.T, XP),
        kernel_table(),
    )
    tables = tuple(jnp.asarray(table) for table in tables)
    flat = (SENT_ROWS, LANES)
    half = (SENT_ROWS // 2, LANES)
    scratch = [pltpu.VMEM((2, 1, POINTS), F32), pltpu.SMEM((4,), jnp.int32), pltpu.SMEM((1, 2), jnp.int32)]
    stays, goes, own, kept, weights = call(
        prelude_kernel, [FAR] * 4, [half] * 2 + [flat] * 2 + [(8, LANES)],
        scratch + [pltpu.VMEM(flat, F32), pltpu.SemaphoreType.DMA((6,))], 1,
    )(occupation_signs, window_offsets, ground_orbitals, response_orbitals)
    count = lax.axis_size("orb")
    visiting = lax.ppermute(kept, "orb", [((i + 1) % count, i) for i in range(count)])
    mine, other = summed_over_devices(stays, goes)
    low_lines, high_lines = lines_call(ground_orbitals)
    coefficient = call(
        coefficient_kernel, [FAR, VECTORS], [flat],
        [pltpu.VMEM((POINTS,), F32), pltpu.SemaphoreType.DMA], 1,
    )(ground_density, own)[0]
    values, partial = first_half(0, weights, low_lines, kept, *tables)
    away_values, away_partial = first_half(1, weights, low_lines, visiting, *tables)
    away = second_half(1, weights, high_lines, visiting, *tables, away_values, away_partial)
    second = lax.ppermute(away, "orb", [(i, (i + 1) % count) for i in range(count)])
    first = second_half(0, weights, high_lines, kept, *tables, values, partial)
    return call(finish_kernel, [VECTORS] * 5, [(1, POINTS)], [pltpu.VMEM(flat, F32)], 1)(
        coefficient, mine, other, first, second
    )[0]


def solution(mesh):
    placed = (P("orb", None), P("orb"), P(("orb", "grid"), None), P(("orb", "grid"), None), P())
    return jax.shard_map(per_device, mesh=mesh, in_specs=placed, out_specs=P(("orb", "grid"), None), check_vma=False)
```

```python
import functools
import math

import numpy as np

import jax
import jax.numpy as jnp
from jax import lax
from jax.experimental import pallas as pl
from jax.experimental.pallas import tpu as pltpu
from jax.sharding import PartitionSpec as P


NX = 30
NY = 45
NZ = 60
SPACING = 0.5
SCREEN = 0.5
XC_COEF = 0.3282
HYBRID = 0.25

F32 = jnp.float32
BF16 = jnp.bfloat16
LANES = 128
POINTS = NX * NY * NZ
XP = 32
YP = 48
XS = XP + 1
YS = YP + 1
LINES = math.lcm(NZ, LANES) // NZ
CHUNKS = math.lcm(NZ, LANES) // LANES
PERIODS = -(-NX * NY // LINES)
LINE_ROWS = PERIODS * LINES
GROUPED = -(-PERIODS // 8) * 8
FLAT_ROWS = GROUPED * CHUNKS
PITCHED_ROWS = GROUPED * (LINES + 1)
WHOLE = POINTS // LANES
TAIL = POINTS - WHOLE * LANES
SENT_ROWS = 640


def real_basis(count):
    waves = np.arange(count)
    folded = np.where(waves <= count // 2, waves, count - waves)
    angle = 2.0 * np.pi * np.outer(folded, waves) / count
    basis = np.where((waves <= count // 2)[:, None], np.cos(angle), np.sin(angle))
    return basis / np.sqrt(np.sum(basis**2, 1, keepdims=True))


def split_table(table):
    table = table.astype(np.float32)
    high = table.astype(jnp.bfloat16)
    return high, (table - high.astype(np.float32)).astype(jnp.bfloat16)


def padded(table, size):
    return np.pad(table, ((0, size - table.shape[0]), (0, size - table.shape[1])))


def lane_table(matrix):
    high, low = (padded(np.kron(np.eye(2, dtype=jnp.bfloat16), part), LANES) for part in split_table(matrix))
    return np.block([[high, low], [high, np.zeros_like(low)]])


def row_table(matrix, size):
    high, low = (padded(part, size) for part in split_table(matrix))
    return np.concatenate([high, high, low], 1)


def kernel_table():
    def squares(count):
        places = np.arange(count)
        folded = np.where(places <= count // 2, places, places - count)
        waves = folded.astype(np.float32) * np.float32(2.0 * math.pi / (count * SPACING))
        return waves * waves

    squared = squares(NX)[None, :, None] + squares(NY)[:, None, None] + squares(NZ)[None, None, :]
    table = np.zeros((YP, XP, LANES), np.float32)
    table[:NY, :NX, : 2 * NZ] = np.tile(4.0 * math.pi / (squared + SCREEN * SCREEN), (1, 1, 2))
    return table.reshape(YP * XP, LANES)


def split(values):
    high = values.astype(BF16)
    return high, (values - high.astype(F32)).astype(BF16)


def lane_product(values, table):
    high, low = split(values)
    halves = []
    for start in range(0, values.shape[1], LANES):
        lanes = slice(start, start + LANES)
        both = jnp.dot(jnp.concatenate([high[:, lanes], low[:, lanes]], 1), table, preferred_element_type=F32)
        halves.append(both[:, :LANES] + both[:, LANES:])
    return jnp.concatenate(halves, 1)


def row_product(table, values):
    high, low = split(values)
    return jnp.dot(table, jnp.concatenate([high, low, high], 0), preferred_element_type=F32)


def lane_ids(rows):
    return lax.broadcasted_iota(jnp.int32, (rows, LANES), 1)


def turned(values, shift):
    shift %= LANES
    return pltpu.roll(values, shift, 1) if shift else values


def two_lines(flat, line, places):
    chunk, start = divmod(NZ * line, LANES)
    value = flat[pl.ds(chunk, PERIODS, stride=CHUNKS), :]
    if start + 2 * NZ > LANES:
        after = flat[pl.ds(chunk + 1, PERIODS, stride=CHUNKS), :]
        value = jnp.where(lane_ids(PERIODS) >= start, value, after)
    return [turned(value, place - start) for place in places]


def to_lines(left, right, lines, pitched):
    ids = lane_ids(PERIODS)
    for line in range(0, LINES, 2):
        if left is right:
            middle, late, early = two_lines(left, line, (0, NZ, -NZ))
            pairs = (jnp.where(ids < NZ, middle, late), jnp.where(ids < NZ, early, middle))
        else:
            (low, next_low), (high, next_high) = two_lines(left, line, (0, -NZ)), two_lines(right, line, (NZ, 0))
            pairs = (jnp.where(ids < NZ, low, high), jnp.where(ids < NZ, next_low, next_high))
        for place, pair in enumerate(pairs):
            pair = jnp.where(ids < 2 * NZ, pair, 0.0)
            pitched[pl.ds(line + place, PERIODS, stride=LINES + 1), :] = pair
    for period in range(PERIODS):
        lines[pl.ds(period * LINES, LINES), :] = pitched[pl.ds(period * (LINES + 1), LINES), :]


def to_flat(lines, flat, pitched):
    ids = lane_ids(PERIODS)
    for period in range(PERIODS):
        pitched[pl.ds(period * (LINES + 1), LINES), :] = lines[pl.ds(period * LINES, LINES), :]
    for chunk in range(CHUNKS):
        low = chunk * LANES
        merged = None
        for line in range(low // NZ, -(-(low + LANES) // NZ)):
            value = turned(pitched[pl.ds(line, PERIODS, stride=LINES + 1), :], NZ * line - low)
            merged = value if merged is None else jnp.where(ids >= NZ * line - low, value, merged)
        flat[pl.ds(chunk, PERIODS, stride=CHUNKS), :] = merged


def body_copy(row, flat, sem):
    target = flat.at[pl.ds(0, WHOLE), :].reshape(1, WHOLE * LANES)
    return pltpu.make_async_copy(row.at[:, pl.ds(0, WHOLE * LANES)], target, sem)


def fill_tail(tail, flat):
    flat[pl.ds(WHOLE, flat.shape[0] - WHOLE), :] = jnp.zeros((flat.shape[0] - WHOLE, LANES), F32)
    flat[pl.ds(WHOLE, 1), pl.ds(0, TAIL)] = tail


def grouped(count, group, body):
    lax.fori_loop(0, count // group, lambda step, carry: (body(step * group), carry)[1], 0)


def prelude_kernel(signs, offsets, ground, response, stays, goes, own, kept, weights, rows, sign, offset, term, sems):
    place = lax.axis_index("grid")
    spot = pl.ds(place, 1)
    copies = [
        pltpu.make_async_copy(signs, sign, sems.at[0]),
        pltpu.make_async_copy(offsets, offset, sems.at[1]),
        body_copy(response, kept, sems.at[2]),
        pltpu.make_async_copy(response, rows.at[0], sems.at[3]),
        body_copy(ground.at[spot, :], own, sems.at[4]),
        pltpu.make_async_copy(ground.at[spot, :], rows.at[1], sems.at[5]),
    ]
    for copy in copies:
        copy.start()
    for copy in copies:
        copy.wait()
    last = pl.ds(WHOLE * LANES, TAIL)
    fill_tail(rows[0, :, last], kept)
    fill_tail(rows[1, :, last], own)
    term[...] = sign[place].astype(F32) * own[...] * kept[...]
    share(term, 1, stays, goes)
    for step in range(2):
        kept[pl.ds(SENT_ROWS - 2 + step, 1), :] = jnp.full((1, LANES), offset[0, step].astype(F32))
    ids = lane_ids(1)
    for half in range(2):
        pair = jnp.where(ids < NZ, sign[2 * half].astype(F32), sign[2 * half + 1].astype(F32))
        weights[pl.ds(half, 1), :] = pair


def lines_kernel(ground, low_lines, high_lines, flats, pitched, sems):
    copies = [body_copy(ground.at[pl.ds(j, 1), :], flats.at[j], sems.at[j]) for j in range(4)]
    for copy in copies:
        copy.start()
    for j in range(4):
        copies[j].wait()
        fill_tail(ground[pl.ds(j, 1), pl.ds(WHOLE * LANES, TAIL)], flats.at[j])
    to_lines(flats.at[0], flats.at[1], low_lines, pitched)
    to_lines(flats.at[2], flats.at[3], high_lines, pitched)


def coefficient_kernel(density, own, coefficient, values, sem):
    copy = pltpu.make_async_copy(density, values, sem)
    copy.start()
    copy.wait()
    block = 8 * LANES
    for start in range(0, POINTS, block):
        size = min(block, POINTS - start)
        shape = (8, LANES) if size == block else (1, size)
        value = values[pl.ds(start, size)].reshape(shape)
        value = -XC_COEF * jnp.exp(jnp.log(value) * (-2.0 / 3.0))
        spot = (pl.ds(start // LANES, shape[0]), pl.ds(0, shape[1]))
        coefficient[spot] = value * own[spot]


def solve_half(half, step, weights, lines, values, response, tables, kernel_copy, scratch, total, prior):
    kernel, waves, turned_waves = scratch
    z_table, z_back, y_table, y_back, x_table, x_back = (table[...] for table in tables)
    for x in range(NX, XP):
        waves[pl.ds(x, YP, stride=XS), :] = jnp.zeros((YP, LANES), F32)
    for y in range(NY, YP):
        turned_waves[pl.ds(y, XP, stride=YS), :] = jnp.zeros((XP, LANES), F32)

    def forward(x):
        group = 15
        spots = [pl.ds((x + u) * NY, YP) for u in range(group)]
        value = lane_product(jnp.concatenate([lines[spot, :] * values[spot, :] for spot in spots], 0), z_table)
        value = row_product(y_table, jnp.concatenate([value[u * YP : (u + 1) * YP] for u in range(group)], 1))
        for u in range(group):
            waves[pl.ds(x + u, YP, stride=XS), :] = value[:, u * LANES : (u + 1) * LANES]

    def middle(y):
        group = 45
        spots = [pl.ds(pl.multiple_of((y + u) * XP, XP), XP) for u in range(group)]
        value = row_product(x_table, jnp.concatenate([waves[pl.ds((y + u) * XS, XP), :] for u in range(group)], 1))
        value = row_product(x_back, value * jnp.concatenate([kernel[spot, :] for spot in spots], 1))
        for u in range(group):
            turned_waves[pl.ds(y + u, XP, stride=YS), :] = value[:, u * LANES : (u + 1) * LANES]

    orbital = 2 * half + (lane_ids(1) >= NZ).astype(jnp.int32)
    offset = response[pl.ds(SENT_ROWS - 2 + step, 1), :]
    factor = jnp.where(orbital.astype(F32) >= offset, weights[pl.ds(half, 1), :], 0.0)

    def backward(x):
        group = 30
        spots = [pl.ds((x + u) * YS, YP) for u in range(group)]
        value = row_product(y_back, jnp.concatenate([turned_waves[spot, :] for spot in spots], 1))
        value = jnp.concatenate([value[:, u * LANES : (u + 1) * LANES] for u in range(group)], 0)
        value = lane_product(value, z_back)
        for u in range(group):
            spot = pl.ds((x + u) * NY, YP)
            part = value[u * YP : (u + 1) * YP] * (lines[spot, :] * factor)
            if prior is not None:
                part += prior[spot, :]
                part += pltpu.roll(part, LANES - NZ, 1)
            total[spot, :] = part

    grouped(NX, 15, forward)
    kernel_copy.wait()
    grouped(NY, 45, middle)
    grouped(NX, 30, backward)


def first_half_kernel(step, weights, lines, response, *refs):
    tables, (kernel, values, partial, flat, pitched, sem, *scratch) = refs[:6], refs[6:]
    kernel_copy = pltpu.make_async_copy(kernel, scratch[0], sem)
    kernel_copy.start()
    flat[pl.ds(0, WHOLE + 1), :] = response[pl.ds(0, WHOLE + 1), :]
    flat[pl.ds(WHOLE + 1, FLAT_ROWS - WHOLE - 1), :] = jnp.zeros((FLAT_ROWS - WHOLE - 1, LANES), F32)
    to_lines(flat, flat, values, pitched)
    solve_half(0, step, weights, lines, values, response, tables, kernel_copy, scratch, partial, None)


def second_half_kernel(step, weights, lines, response, *refs):
    tables, (kernel, values, partial, exchange, flat, pitched, sem, *scratch, total) = refs[:6], refs[6:]
    kernel_copy = pltpu.make_async_copy(kernel, scratch[0], sem)
    kernel_copy.start()
    solve_half(1, step, weights, lines, values, response, tables, kernel_copy, scratch, total, partial)
    to_flat(total, flat, pitched)
    exchange[...] = flat[pl.ds(0, SENT_ROWS), :]


def finish_kernel(coefficient, mine, other, first, second, out, density):
    join_kernel(1, mine, other, density)
    value = coefficient[...] * density[...] - HYBRID * (first[...] + second[...])
    out.at[:, pl.ds(0, WHOLE * LANES)].reshape(WHOLE, LANES)[...] = value[:WHOLE]
    out[:, pl.ds(WHOLE * LANES, TAIL)] = value[WHOLE : WHOLE + 1, :TAIL]


SCALARS = pl.BlockSpec(memory_space=pltpu.SMEM)
VECTORS = pl.BlockSpec(memory_space=pltpu.VMEM)
FAR = pl.BlockSpec(memory_space=pltpu.HBM)


def near(shape):
    return pltpu.VMEM(shape, F32) if shape != (1, POINTS) else jax.ShapeDtypeStruct(shape, F32)


def placed(values, spec):
    space = {id(FAR): pltpu.HBM, id(VECTORS): pltpu.VMEM}.get(id(spec))
    return values if space is None else pltpu.with_memory_space_constraint(values, space)


def call(body, specs, shapes, scratch, microseconds):
    cost = pl.CostEstimate(flops=int(microseconds * 1e9), bytes_accessed=int(microseconds * 1e6), transcendentals=0)
    kernel = pl.pallas_call(
        body,
        in_specs=specs,
        out_shape=[near(shape) for shape in shapes],
        out_specs=[VECTORS] * len(shapes),
        scratch_shapes=scratch,
        cost_estimate=cost,
        compiler_params=pltpu.CompilerParams(vmem_limit_bytes=12 * 2**20),
    )
    return lambda *values: kernel(*(placed(v, spec) for spec, v in zip(specs, values)))


def orb_bit(distance):
    return lax.rem(lax.div(lax.axis_index("orb"), distance), 2)


def share(term, distance, stays, goes):
    half, bit = stays.shape[0], orb_bit(distance)
    stays[...] = term[pl.ds(pl.multiple_of(bit * half, half), half), :]
    goes[...] = term[pl.ds(pl.multiple_of((1 - bit) * half, half), half), :]


def add_kernel(mine, other, out):
    out[...] = mine[...] + other[...]


def join_kernel(distance, mine, other, out):
    half, bit = mine.shape[0], orb_bit(distance)
    out[pl.ds(pl.multiple_of(bit * half, half), half), :] = mine[...]
    out[pl.ds(pl.multiple_of((1 - bit) * half, half), half), :] = other[...]


def swap(values, partner):
    orbs, grids = lax.axis_size("orb"), lax.axis_size("grid")
    pairs = []
    for orb in range(orbs):
        for grid in range(grids):
            axis, distance = partner(orb)
            to = (orb ^ distance, grid) if axis == "orb" else (orb, grid ^ distance)
            pairs.append((orb * grids + grid, to[0] * grids + to[1]))
    return lax.ppermute(values, ("orb", "grid"), pairs)


def added(mine, other):
    return call(add_kernel, [VECTORS] * 2, [mine.shape], [], 0.1)(mine, other)[0]


def summed_over_devices(stays, goes):
    steps = [("orb", 1 << bit) for bit in range(1, lax.axis_size("orb").bit_length() - 1)]
    steps += [("grid", 1 << bit) for bit in range(lax.axis_size("grid").bit_length() - 1)]
    turn = len(steps) // 2
    orders = (steps, steps[turn:] + steps[:turn])
    other = swap(goes, lambda orb: ("orb", 1))
    term = added(stays, other)
    for place in range(len(steps)):
        other = swap(term, lambda orb: orders[orb % 2][place])
        term = added(term, other)
    return term, swap(term, lambda orb: ("orb", 1))


def half_call(body, step, shapes, extra, values):
    flat, pitched = pltpu.VMEM((FLAT_ROWS, LANES), F32), pltpu.VMEM((PITCHED_ROWS, LANES), F32)
    scratch = [flat, pitched, pltpu.SemaphoreType.DMA, pltpu.VMEM((YP * XP, LANES), F32)]
    scratch += [pltpu.VMEM((YP * XS, LANES), F32), pltpu.VMEM((XP * YS, LANES), F32)] + extra
    specs = [VECTORS] * 9 + [FAR] + [VECTORS] * (len(values) - 10)
    return call(functools.partial(body, step), specs, shapes, scratch, 3)(*values)


def first_half(step, *shared):
    return half_call(first_half_kernel, step, [(LINE_ROWS, LANES)] * 2, [], shared)


def second_half(step, *shared):
    line = pltpu.VMEM((LINE_ROWS, LANES), F32)
    return half_call(second_half_kernel, step, [(SENT_ROWS, LANES)], [line], shared)[0]


def lines_call(ground):
    return call(
        lines_kernel, [VECTORS], [(LINE_ROWS, LANES)] * 2,
        [pltpu.VMEM((4, FLAT_ROWS, LANES), F32), pltpu.VMEM((PITCHED_ROWS, LANES), F32),
         pltpu.SemaphoreType.DMA((4,))], 2,
    )(ground)


def per_device(ground_orbitals, occupation_signs, response_orbitals, window_offsets, ground_density):
    assert ground_orbitals.shape == (4, POINTS) and response_orbitals.shape[0] == 1
    basis_x, basis_y, basis_z = real_basis(NX), real_basis(NY), real_basis(NZ)
    tables = (
        lane_table(basis_z.T), lane_table(basis_z),
        row_table(basis_y, YP), row_table(basis_y.T, YP),
        row_table(basis_x, XP), row_table(basis_x.T, XP),
        kernel_table(),
    )
    tables = tuple(jnp.asarray(table) for table in tables)
    flat = (SENT_ROWS, LANES)
    half = (SENT_ROWS // 2, LANES)
    scratch = [pltpu.VMEM((2, 1, POINTS), F32), pltpu.SMEM((4,), jnp.int32), pltpu.SMEM((1, 2), jnp.int32)]
    stays, goes, own, kept, weights = call(
        prelude_kernel, [FAR] * 4, [half] * 2 + [flat] * 2 + [(8, LANES)],
        scratch + [pltpu.VMEM(flat, F32), pltpu.SemaphoreType.DMA((6,))], 1,
    )(occupation_signs, window_offsets, ground_orbitals, response_orbitals)
    count = lax.axis_size("orb")
    visiting = lax.ppermute(kept, "orb", [((i + 1) % count, i) for i in range(count)])
    mine, other = summed_over_devices(stays, goes)
    low_lines, high_lines = lines_call(ground_orbitals)
    coefficient = call(
        coefficient_kernel, [FAR, VECTORS], [flat],
        [pltpu.VMEM((POINTS,), F32), pltpu.SemaphoreType.DMA], 1,
    )(ground_density, own)[0]
    values, partial = first_half(0, weights, low_lines, kept, *tables)
    away_values, away_partial = first_half(1, weights, low_lines, visiting, *tables)
    away = second_half(1, weights, high_lines, visiting, *tables, away_values, away_partial)
    second = lax.ppermute(away, "orb", [(i, (i + 1) % count) for i in range(count)])
    first = second_half(0, weights, high_lines, kept, *tables, values, partial)
    return call(finish_kernel, [VECTORS] * 5, [(1, POINTS)], [pltpu.VMEM(flat, F32)], 1)(
        coefficient, mine, other, first, second
    )[0]


def solution(mesh):
    placed = (P("orb", None), P("orb"), P(("orb", "grid"), None), P(("orb", "grid"), None), P())
    return jax.shard_map(per_device, mesh=mesh, in_specs=placed, out_specs=P(("orb", "grid"), None), check_vma=False)
```
